32 devices in a mesh: groups: 2 (over y), blk: 4 (over z), layer: 2 (over x), rep: 2 (over core).
Axes of the slice: x: 2, y: 2, z: 4, core: 2. Of those that a mesh axis runs over, the one named last changes fastest.
Arguments:
- train_grads: bfloat16 [2, 8192, 4096], P('layer', ('groups', 'blk')), parts along dimension 1, may hold values from -0.29882812 to 0.29882812
- queries: bfloat16 [2, 2, 512, 4096], P('layer', 'rep', ('groups', 'blk')), parts along dimension 2, may hold values from -0.59765625 to 0.59765625
- bases: bfloat16 [2, 64, 128], P('layer', ('blk', 'rep')), may hold values from -0.75 to 0.75
- eigenvalues: float32 [2, 4096], P('layer', ('blk', 'rep')), may hold values from 0.01 to 10
Outputs:
- scores: float32 [2, 256, 8192], P('rep', 'layer', ('groups', 'blk')), parts along dimension 2
The draws below stay inside these ranges and needn't reach their ends.
There are 2 independent parts, one for each index of `groups`. The reference program is written for one: setup_inputs(seed, part) draws one part's arguments, and reference() takes and returns one part's arrays. A program takes and returns all parts, laid end to end along the dimension named above; an argument that names none is the same for every part. Nothing has to cross between parts.
All inputs are finite; a program needn't handle non-finite values.
Results may differ from the reference program's by a relative error of at most 0.0042.
Values may be sent and summed in bfloat16 or wider, within the bound.
No kernel may reach another device: no remote copies, remote signals or barrier semaphores. Data moves between devices by JAX's collectives and lax.ppermute only.
A program may use at most 128 MiB of HBM per device.

```python
import math
import jax
import jax.numpy as jnp
from jax import lax

K = 64
P_SIZE = 4096
L = 2
QH = 256
NT = 4096
N_REP = 2


def block_scale(key, extent, split, low, top_value):
    def one(axis_at, blocks):
        draws = jax.random.uniform(jax.random.fold_in(jax.random.fold_in(key, 6), axis_at), (blocks,), jnp.float32, low / len(split), top_value / len(split))
        return jnp.repeat(jnp.exp(draws), extent[axis_at] // blocks).reshape((-1,) + (1,) * (len(extent) - axis_at - 1))

    loudness = one(*split[0])
    for cut in split[1:]:
        loudness = loudness * one(*cut)
    return loudness


def scatter_about(stream_key, extent, width, limit, split=(), held_as=jnp.bfloat16):
    values = width * jax.random.normal(stream_key, extent, jnp.float32)
    if split:
        values = values * block_scale(stream_key, extent, split, -0.22, 0.18)
    return jnp.clip(values, -limit, limit).astype(held_as)


def setup_inputs(seed: int = 0, part: int = 0) -> dict:
    keys = jax.random.split(jax.random.key(seed), 5)
    part_splits = jax.random.split(jax.random.fold_in(keys[4], part), 5)
    train_grads = scatter_about(part_splits[0], (L, NT, P_SIZE), 0.05, 0.29882812, ((0, 2), (1, 4)))
    queries = scatter_about(part_splits[1], (L, N_REP, QH, P_SIZE), 0.1, 0.59765625, ((0, 2), (1, 2), (2, 4)))
    bases = scatter_about(keys[2], (L, K, 2 * K), K ** -0.5, 0.75, ((0, 2), (1, 8)))
    eigenvalues = jnp.clip(jnp.exp(math.log(10.0) - 6.9077553 * jax.random.uniform(keys[3], (L, P_SIZE), jnp.float32) ** block_scale(keys[3], (L, P_SIZE), ((0, 2), (1, 8)), -0.2, 0.2)), 0.01, 10.0)
    return {"train_grads": train_grads, "queries": queries, "bases": bases, "eigenvalues": eigenvalues}


def rotate_rows(grads, basis):
    factor_size = basis.shape[0]
    row_count = grads.shape[0]
    grad_square = grads.astype(jnp.float32).reshape(row_count, factor_size, factor_size)
    right_basis = basis[:, factor_size:].astype(jnp.float32)
    left_basis = basis[:, :factor_size].astype(jnp.float32)
    half_turn = jnp.einsum('rab,bc->rac', grad_square, right_basis).astype(jnp.bfloat16)
    half_turn = lax.optimization_barrier(half_turn)
    full_turn = jnp.einsum('ca,rcb->rab', left_basis, half_turn.astype(jnp.float32))
    return full_turn.reshape(row_count, factor_size * factor_size)


def reference(train_grads, queries, bases, eigenvalues):
    layer_count = train_grads.shape[0]
    query_rows = queries.reshape(layer_count, queries.shape[1] * queries.shape[2], queries.shape[3])
    score_sum = jnp.zeros((query_rows.shape[1], train_grads.shape[1]), jnp.float32)
    for layer_index in range(layer_count):
        eigen_row = eigenvalues[layer_index]
        inverse_damped = 1.0 / (eigen_row + 0.1 * jnp.mean(eigen_row))
        train_turned = rotate_rows(train_grads[layer_index], bases[layer_index]).astype(jnp.bfloat16)
        query_turned = (rotate_rows(query_rows[layer_index], bases[layer_index]) * inverse_damped).astype(jnp.bfloat16)
        score_sum = score_sum + jnp.dot(query_turned, train_turned.T, preferred_element_type=jnp.float32)
    return score_sum.reshape(queries.shape[1], queries.shape[2], train_grads.shape[1])
```

```python
import jax
import jax.numpy as jnp
from jax import lax
from jax.sharding import PartitionSpec as P


def line_plan(count):
    plan, arrivals = {}, [[] for _ in range(count)]
    for step in range(1, count):
        for parity in range(2):
            pairs = []
            for low in range(parity, count - 1, 2):
                high = low + 1
                if low - (step - 1) >= 0:
                    pairs.append((low, high))
                    arrivals[high].append((step, parity, low - (step - 1)))
                if high + (step - 1) < count:
                    pairs.append((high, low))
                    arrivals[low].append((step, parity, high + (step - 1)))
            if pairs:
                plan[step, parity] = pairs
    return plan, arrivals


def table(values, index):
    return jnp.asarray(values, jnp.int32)[index]


def query_weights(rows, left, right, inverse_damped):
    factor = left.shape[0]
    square = rows.reshape(-1, factor, factor)
    half = jnp.einsum("rab,bc->rac", square, right, preferred_element_type=jnp.float32)
    turned = jnp.einsum(
        "ca,rcb->rab", left, half.astype(jnp.bfloat16), preferred_element_type=jnp.float32
    )
    scaled = (turned * inverse_damped.reshape(1, factor, factor)).astype(jnp.bfloat16)
    back = jnp.einsum("ca,rab->rcb", left, scaled, preferred_element_type=jnp.float32)
    weights = jnp.einsum(
        "rab,cb->rac", back.astype(jnp.bfloat16), right, preferred_element_type=jnp.float32
    )
    return weights.astype(jnp.bfloat16).reshape(rows.shape)


def body(train_grads, queries, bases, eigenvalues):
    blocks, layers = lax.axis_size("blk"), lax.axis_size("layer")
    z, x = lax.axis_index("blk"), lax.axis_index("layer")
    train = train_grads[0]
    own = queries[0, 0]
    factor = bases.shape[2] // 2
    packed = jnp.concatenate(
        [bases[0].astype(jnp.float32), eigenvalues.reshape(-1, 2 * factor)], axis=0
    )
    gathered = lax.all_gather(packed, ("blk", "rep"), axis=0)
    base_rows = bases.shape[1]
    basis = gathered[:, :base_rows].reshape(factor, 2 * factor).astype(jnp.bfloat16)
    eigen = gathered[:, base_rows:].reshape(-1)
    left, right = basis[:, :factor], basis[:, factor:]
    inverse_damped = 1.0 / (eigen + 0.1 * jnp.mean(eigen))

    plan, arrivals = line_plan(blocks)
    results = {(0, 0): own, (0, 1): own}
    for (step, parity), pairs in plan.items():
        results[step, parity] = lax.ppermute(results[step - 1, 1 - parity], "blk", pairs)

    per_owner = blocks // layers
    partials, totals, places = [], [], []
    for j in range(blocks):
        if j == 0:
            rows, block_of = own, list(range(blocks))
        else:
            sources = [a[j - 1][:2] for a in arrivals]
            block_of = [a[j - 1][2] for a in arrivals]
            names = sorted(set(sources))
            which = table([names.index(s) for s in sources], z)
            rows = results[names[0]]
            for i, name in enumerate(names[1:], 1):
                rows = jnp.where(which == i, results[name], rows)
        weights = query_weights(rows, left, right, inverse_damped)
        partial = jnp.einsum("qp,tp->qt", weights, train, preferred_element_type=jnp.float32)
        total = partial
        for shift in range(1, layers):
            pairs = []
            for at in range(blocks):
                owner = block_of[at] // per_owner
                pairs.append((at * layers + (owner - shift) % layers, at * layers + owner))
            total = total + lax.ppermute(partial, ("blk", "layer"), pairs)
        totals.append(total)
        places.append(block_of)
    outputs = []
    for m in range(per_owner):
        block = x * per_owner + m
        value = totals[0]
        for j in range(1, blocks):
            value = jnp.where(table(places[j], z) == block, totals[j], value)
        outputs.append(value)
    return jnp.concatenate(outputs, axis=0)[None]


def solution(mesh):
    return jax.shard_map(
        body,
        mesh=mesh,
        in_specs=(
            P("layer", ("groups", "blk"), None),
            P("layer", "rep", ("groups", "blk"), None),
            P("layer", ("blk", "rep"), None),
            P("layer", ("blk", "rep")),
        ),
        out_specs=P("rep", "layer", ("groups", "blk")),
        check_vma=False,
    )
```

```python
import functools

import jax
import jax.numpy as jnp
from jax import lax
from jax.experimental import pallas as pl
from jax.experimental.pallas import tpu as pltpu
from jax.sharding import PartitionSpec as P

TILE = 16
GROUP = 4
BF16, F32 = jnp.bfloat16, jnp.float32
IN_VMEM = pl.BlockSpec(memory_space=pltpu.VMEM)
IN_SMEM = pl.BlockSpec(memory_space=pltpu.SMEM)


def dot(a, b):
    return jnp.dot(a, b, preferred_element_type=F32)


def call(kernel, out_shape, in_specs, scratch, args, flops, grant):
    outs = out_shape if isinstance(out_shape, (list, tuple)) else [out_shape]
    moved = sum(a.size * a.dtype.itemsize for a in list(args) + list(outs))
    return pl.pallas_call(
        kernel,
        out_shape=out_shape,
        in_specs=in_specs,
        out_specs=jax.tree.map(lambda _: IN_VMEM, out_shape),
        scratch_shapes=scratch,
        compiler_params=pltpu.CompilerParams(vmem_limit_bytes=grant),
        cost_estimate=pl.CostEstimate(flops=flops, bytes_accessed=moved, transcendentals=0),
    )(*args)


def line_plan(count):
    plan, arrivals = {}, [[] for _ in range(count)]
    for step in range(1, count):
        for parity in range(2):
            pairs = []
            for low in range(parity, count - 1, 2):
                high = low + 1
                if low - (step - 1) >= 0:
                    pairs.append((low, high))
                    arrivals[high].append((step, parity, low - (step - 1)))
                if high + (step - 1) < count:
                    pairs.append((high, low))
                    arrivals[low].append((step, parity, high + (step - 1)))
            if pairs:
                plan[step, parity] = pairs
    return plan, arrivals


def lookup(values, index):
    value = jnp.int32(values[0])
    for i, v in enumerate(values[1:], 1):
        if v != values[0]:
            value = jnp.where(index == i, jnp.int32(v), value)
    return value


def spread(matrix, rows, cols, keep):
    size = matrix.shape[0]
    r = lax.broadcasted_iota(jnp.int32, (rows, size), 0)
    i = lax.broadcasted_iota(jnp.int32, (rows, size), 1)
    j = lax.broadcasted_iota(jnp.int32, (size, cols), 0)
    c = lax.broadcasted_iota(jnp.int32, (size, cols), 1)
    down = jnp.where(lax.rem(r, size) == i, 1.0, 0.0).astype(BF16)
    along = jnp.where(lax.rem(c, size) == j, 1.0, 0.0).astype(BF16)
    full = dot(dot(down, matrix.astype(BF16)).astype(BF16), along)
    block_row = lax.broadcasted_iota(jnp.int32, (rows, cols), 0) // size
    block_col = lax.broadcasted_iota(jnp.int32, (rows, cols), 1) // size
    return jnp.where(keep(block_row, block_col), full, 0.0).astype(BF16)


def prep_kernel(shape, here_ref, *refs):
    count, reps, base_rows, eigen_rows, fold = shape
    parts = refs[:count]
    w1_ref, but_ref, bu_ref, w5_ref, inv_ref, base3, eigen3, base, eigen, pad = refs[count:]
    z, rep = here_ref[0], here_ref[2]
    each = base_rows + eigen_rows
    for d in range(count):
        for e in range(reps):
            source = lax.rem(z + count - d, count) * reps + lax.rem(rep + reps - e, reps)
            base3[source] = parts[d][e * each : e * each + base_rows, :]
            eigen3[source] = parts[d][e * each + base_rows : (e + 1) * each, :]
    for s in range(count * reps):
        base[s * base_rows : (s + 1) * base_rows, :] = base3[s]
        eigen[s * eigen_rows : (s + 1) * eigen_rows, :] = eigen3[s]
    size = base.shape[0]
    basis = base[...]
    left, right = basis[:, :size], basis[:, size:]
    turned = basis.T
    left_t, right_t = turned[:size], turned[size:]
    wide = 2 * size * fold
    same = lambda r, c: r == c
    w1_ref[...] = spread(
        right, wide, wide, lambda r, c: (r // 2 == lax.rem(c, fold)) & (lax.rem(r, 2) == c // fold)
    )
    w5_ref[...] = spread(
        right_t, wide, wide, lambda r, c: (c // 2 == lax.rem(r, fold)) & (lax.rem(c, 2) == r // fold)
    )
    but_ref[...] = spread(left_t, GROUP * size, GROUP * size, same)
    bu_ref[...] = spread(left, GROUP * size, GROUP * size, same)
    values = eigen[...]
    inverse = 1.0 / (values + 0.1 * (jnp.sum(values) / (size * size)))
    shifted = pltpu.roll(inverse, size, 1)
    lane = lax.broadcasted_iota(jnp.int32, inverse.shape, 1)
    pad[pl.ds(0, size // 2, stride=2), :] = jnp.where(lane < size, inverse, shifted)
    pad[pl.ds(1, size // 2, stride=2), :] = jnp.where(lane < size, shifted, inverse)
    for g in range(GROUP):
        for h in range(fold // 2):
            inv_ref[g * size : (g + 1) * size, h * 2 * size : (h + 1) * 2 * size] = pad[...]


def rotation_constants(parts, here, reps, base_rows, eigen_rows, size, fold):
    count = len(parts)
    wide, tall = 2 * size * fold, GROUP * size
    shard = count * reps
    return call(
        functools.partial(prep_kernel, (count, reps, base_rows, eigen_rows, fold)),
        [
            jax.ShapeDtypeStruct((wide, wide), BF16),
            jax.ShapeDtypeStruct((tall, tall), BF16),
            jax.ShapeDtypeStruct((tall, tall), BF16),
            jax.ShapeDtypeStruct((wide, wide), BF16),
            jax.ShapeDtypeStruct((tall, size * fold), F32),
        ],
        [IN_SMEM] + [IN_VMEM] * count,
        [
            pltpu.VMEM((shard, base_rows, 2 * size), F32),
            pltpu.VMEM((shard, eigen_rows, 2 * size), F32),
            pltpu.VMEM((size, 2 * size), F32),
            pltpu.VMEM((size // 2, 2 * size), F32),
            pltpu.VMEM((size, 2 * size), F32),
        ],
        (here, *parts),
        flops=2 * wide * wide * 2 * size,
        grant=12 << 20,
    )


def rotate_kernel(sources, choice, splits, here_ref, *refs):
    inputs, refs = refs[:sources], refs[sources:]
    w1_ref, but_ref, bu_ref, w5_ref, inv_ref = refs[:5]
    outs = refs[5 : 6 + splits]
    tall = refs[6 + splits]
    scratch = refs[7 + splits :]
    first, second = scratch[: len(scratch) // 2], scratch[len(scratch) // 2 :]
    fold = inputs[0].shape[0] // TILE
    lanes = w1_ref.shape[0] // fold
    size = lanes // 2
    pairs = size // 2
    half = size * fold

    def gather_rows(q_ref):
        for a in range(pairs):
            for h in range(fold):
                tall[a * TILE : (a + 1) * TILE, h * lanes : (h + 1) * lanes] = q_ref[
                    h * TILE : (h + 1) * TILE, a * lanes : (a + 1) * lanes
                ]

    if sources == 1:
        gather_rows(inputs[0])
    else:
        which = lookup(choice, here_ref[0])
        for i in range(sources):
            pl.when(which == i)(functools.partial(gather_rows, inputs[i]))
    chunk = 8
    for a0 in range(0, pairs, chunk):
        rows = dot(tall[a0 * TILE : (a0 + chunk) * TILE, :], w1_ref[...])
        for a in range(a0, a0 + chunk):
            piece = rows[(a - a0) * TILE : (a - a0 + 1) * TILE]
            for c, ref in enumerate(first):
                low = c * lanes
                ref[pl.ds(2 * a, TILE, stride=size), :] = piece[:, low : low + lanes]
                ref[pl.ds(2 * a + 1, TILE, stride=size), :] = piece[:, half + low : half + low + lanes]
    but, bu, inverse = but_ref[...], bu_ref[...], inv_ref[...]
    step = GROUP * size
    for g in range(TILE // GROUP):
        part = jnp.concatenate([ref[g * step : (g + 1) * step, :].astype(BF16) for ref in first], axis=1)
        scaled = (dot(but, part) * inverse).astype(BF16)
        back = dot(bu, scaled)
        for c, ref in enumerate(second):
            ref[g * step : (g + 1) * step, :] = back[:, c * lanes : (c + 1) * lanes]
    for a in range(pairs):
        for odd in range(2):
            for c, ref in enumerate(second):
                low = odd * half + c * lanes
                tall[a * TILE : (a + 1) * TILE, low : low + lanes] = ref[
                    pl.ds(2 * a + odd, TILE, stride=size), :
                ].astype(BF16)
    for a0 in range(0, pairs, chunk):
        rows = dot(tall[a0 * TILE : (a0 + chunk) * TILE, :], w5_ref[...]).astype(BF16)
        for a in range(a0, a0 + chunk):
            for h in range(fold):
                value = rows[(a - a0) * TILE : (a - a0 + 1) * TILE, h * lanes : (h + 1) * lanes]
                outs[0][h * TILE : (h + 1) * TILE, a * lanes : (a + 1) * lanes] = value
                if splits:
                    per = fold // splits
                    low = (h % per) * TILE
                    outs[1 + h // per][low : low + TILE, a * lanes : (a + 1) * lanes] = value


def rotate(here, choice, inputs, constants, splits=0):
    rows, width = inputs[0].shape
    fold = rows // TILE
    wide = constants[0].shape[0]
    size = wide // (2 * fold)
    shapes = [jax.ShapeDtypeStruct((rows, width), BF16)]
    shapes += [jax.ShapeDtypeStruct((rows // splits, width), BF16)] * splits if splits else []
    return call(
        functools.partial(rotate_kernel, len(inputs), choice, splits),
        shapes,
        [IN_SMEM] + [IN_VMEM] * (len(inputs) + 5),
        [
            pltpu.VMEM((size // 2 * TILE, wide), BF16),
            *[pltpu.VMEM((TILE * size, 2 * size), F32)] * fold,
        ],
        (here, *inputs, *constants),
        flops=8 * rows * width * size * fold,
        grant=12 << 20,
    )


def score_kernel(shape, here_ref, *refs):
    refs = list(refs)
    units = [[refs.pop(0) for _ in choices] for choices, _ in shape]
    x_ref, kept_ref, sent_ref, held = refs
    at = 0
    for u, candidates in enumerate(units):
        rows = candidates[0].shape[0]

        def take(ref, at=at, rows=rows):
            held[at : at + rows, :] = ref[...]

        if len(candidates) == 1:
            take(candidates[0])
        else:
            which = lookup(shape[u][1], here_ref[0])
            for i, ref in enumerate(candidates):
                pl.when(which == i)(functools.partial(take, ref))
        at += rows
    total = x_ref.shape[0]
    step = min(256, total)
    for t in range(0, total, step):
        value = lax.dot_general(
            x_ref[t : t + step, :], held[...], (((1,), (1,)), ((), ())), preferred_element_type=F32
        ).T
        kept_ref[:, t : t + step] = value
        sent_ref[:, t : t + step] = value.astype(BF16)


def score(here, units, selectors, train):
    rows = sum(u[0].shape[0] for u in units)
    total, width = train.shape
    flat = [w for u in units for w in u]
    return call(
        functools.partial(score_kernel, [(range(len(u)), s) for u, s in zip(units, selectors)]),
        [jax.ShapeDtypeStruct((rows, total), F32), jax.ShapeDtypeStruct((rows, total), BF16)],
        [IN_SMEM] + [IN_VMEM] * (len(flat) + 1),
        [pltpu.VMEM((rows, width), BF16)],
        (here, *flat, train),
        flops=2 * rows * total * width,
        grant=12 << 20,
    )


def finish_kernel(shape, here_ref, *refs):
    refs = list(refs)
    out_ref = refs.pop()
    z, x = here_ref[0], here_ref[1]
    for owners, units, received in shape:
        kept, others = refs.pop(0), [refs.pop(0) for _ in range(received)]

        @pl.when(lookup(owners, z) == x)
        def _(kept=kept, others=others, units=units):
            at = 0
            for rows, places in units:
                value = kept[at : at + rows, :]
                for other in others:
                    value = value + other[at : at + rows, :].astype(F32)
                place = lookup(places, z)
                out_ref[pl.ds(pl.multiple_of(place * rows, rows), rows), :] = value
                at += rows


def load_kernel(x_ref, out_ref, sem):
    pieces = sem.shape[0]
    step = x_ref.shape[0] // pieces
    copies = []
    for i in range(pieces):
        rows = pl.ds(i * step, step)
        copies.append(pltpu.make_async_copy(x_ref.at[rows], out_ref.at[rows], sem.at[i]))
    for copy in copies:
        copy.start()
    for copy in copies:
        copy.wait()


def resident(x):
    return pl.pallas_call(
        load_kernel,
        out_shape=pltpu.VMEM(x.shape, x.dtype),
        in_specs=[pl.BlockSpec(memory_space=pltpu.HBM)],
        out_specs=IN_VMEM,
        scratch_shapes=[pltpu.SemaphoreType.DMA((8,))],
        compiler_params=pltpu.CompilerParams(vmem_limit_bytes=12 << 20),
        cost_estimate=pl.CostEstimate(
            flops=0, bytes_accessed=2 * x.size * x.dtype.itemsize, transcendentals=0
        ),
    )(x)


def body(train_grads, queries, bases, eigenvalues):
    blocks, layers, reps = lax.axis_size("blk"), lax.axis_size("layer"), lax.axis_size("rep")
    z, x, rep = lax.axis_index("blk"), lax.axis_index("layer"), lax.axis_index("rep")
    train = train_grads[0]
    own = queries[0, 0]
    base_rows, lanes = bases.shape[1:]
    size = lanes // 2
    rows = own.shape[0]
    fold = rows // TILE
    per_owner = blocks // layers

    plan, arrivals = line_plan(blocks)
    here = jnp.stack([z, x, rep]).astype(jnp.int32)
    splits = 2

    raw, turned = {}, {}
    raw[1, 1] = lax.ppermute(own, "blk", plan[1, 1])
    raw[1, 0] = lax.ppermute(own, "blk", plan[1, 0])

    eigen = eigenvalues.reshape(-1, lanes)
    eigen_rows = eigen.shape[0]
    packed = jnp.concatenate([bases[0].astype(F32), eigen], axis=0)
    pair = [packed]
    for e in range(1, reps):
        pair.append(lax.ppermute(packed, "rep", [(r, (r + e) % reps) for r in range(reps)]))
    pair = jnp.concatenate(pair, axis=0)
    parts = [pair]
    for d in range(1, blocks):
        parts.append(lax.ppermute(pair, "blk", [(a, (a + d) % blocks) for a in range(blocks)]))
    train, _ = lax.optimization_barrier((train, pair))
    train = resident(train)
    raw[1, 1], train = lax.optimization_barrier((raw[1, 1], train))
    raw[2, 0] = lax.ppermute(raw[1, 1], "blk", plan[2, 0])

    constants = rotation_constants(parts, here, reps, base_rows, eigen_rows, size, fold)
    alone = [0] * blocks
    whole_first, *turned[1, 0] = rotate(here, alone, [raw[1, 0]], constants, splits)
    whole_own, = rotate(here, alone, [own], constants)

    block_of = [list(range(blocks))] + [[a[j][2] for a in arrivals] for j in range(blocks - 1)]
    source_of = [None] + [[a[j][:2] for a in arrivals] for j in range(blocks - 1)]
    finish_args, finish_shape = [], []

    def exchange(units, selectors, names):
        kept, sent = score(here, units, selectors, train)
        owners = [block // per_owner for block in block_of[names[0][0]]]
        received = []
        for shift in range(1, layers):
            pairs = [(a * layers + (o - shift) % layers, a * layers + o) for a, o in enumerate(owners)]
            received.append(lax.ppermute(sent, ("blk", "layer"), pairs))
        finish_args.extend([kept, *received])
        heights = [u[0].shape[0] for u in units]
        places = [
            (height, [b % per_owner * (rows // height) + piece for b in block_of[j]])
            for (j, piece), height in zip(names, heights)
        ]
        finish_shape.append((owners, places, len(received)))
        return sent

    done = exchange([[whole_own], [whole_first]], [alone, alone], [(0, 0), (1, 0)])
    for step, parity in plan:
        if step == 1 or (step, parity) in raw:
            continue
        before = (step - 1, 1 - parity)
        if before not in turned:
            turned[before] = rotate(here, alone, [raw[before]], constants, splits)[1:]
        pieces = turned[before]
        if step > 2:
            pieces = [lax.optimization_barrier((w, done))[0] for w in pieces]
        turned[step, parity] = [lax.ppermute(w, "blk", plan[step, parity]) for w in pieces]

    for j in range(2, blocks):
        names = sorted(set(source_of[j]))
        fresh = [n for n in names if n in raw and n not in turned]
        ready = [n for n in names if n not in fresh]
        if fresh:
            choice = [fresh.index(s) if s in fresh else 0 for s in source_of[j]]
            wide = rotate(here, choice, [raw[n] for n in fresh], constants, splits if ready else 0)
        if not ready:
            exchange([[wide[0]]], [alone], [(j, 0)])
            continue
        for piece in range(splits):
            candidates = [wide[1 + piece]] if fresh else []
            offset = len(candidates)
            candidates += [turned[n][piece] for n in ready]
            selector = [0 if s in fresh else offset + ready.index(s) for s in source_of[j]]
            exchange([candidates], [selector], [(j, piece)])

    out = call(
        functools.partial(finish_kernel, finish_shape),
        jax.ShapeDtypeStruct((per_owner * rows, train.shape[0]), F32),
        [IN_SMEM] + [IN_VMEM] * len(finish_args),
        [],
        (here, *finish_args),
        flops=per_owner * rows * train.shape[0],
        grant=16 << 20,
    )
    return out[None]


def solution(mesh):
    return jax.shard_map(
        body,
        mesh=mesh,
        in_specs=(
            P("layer", ("groups", "blk"), None),
            P("layer", "rep", ("groups", "blk"), None),
            P("layer", ("blk", "rep"), None),
            P("layer", ("blk", "rep")),
        ),
        out_specs=P("rep", "layer", ("groups", "blk")),
        check_vma=False,
    )
```

```python
import functools

import jax
import jax.numpy as jnp
from jax import lax
from jax.experimental import pallas as pl
from jax.experimental.pallas import tpu as pltpu
from jax.sharding import PartitionSpec as P

TILE = 16
GROUP = 4
BF16, F32 = jnp.bfloat16, jnp.float32
IN_VMEM = pl.BlockSpec(memory_space=pltpu.VMEM)
IN_SMEM = pl.BlockSpec(memory_space=pltpu.SMEM)


def dot(a, b):
    return jnp.dot(a, b, preferred_element_type=F32)


def call(kernel, out_shape, in_specs, scratch, args, flops, grant):
    outs = out_shape if isinstance(out_shape, (list, tuple)) else [out_shape]
    moved = sum(a.size * a.dtype.itemsize for a in list(args) + list(outs))
    return pl.pallas_call(
        kernel,
        out_shape=out_shape,
        in_specs=in_specs,
        out_specs=jax.tree.map(lambda _: IN_VMEM, out_shape),
        scratch_shapes=scratch,
        compiler_params=pltpu.CompilerParams(vmem_limit_bytes=grant),
        cost_estimate=pl.CostEstimate(flops=flops, bytes_accessed=moved, transcendentals=0),
    )(*args)


def line_plan(count):
    plan, arrivals = {}, [[] for _ in range(count)]
    for step in range(1, count):
        for parity in range(2):
            pairs = []
            for low in range(parity, count - 1, 2):
                high = low + 1
                if low - (step - 1) >= 0:
                    pairs.append((low, high))
                    arrivals[high].append((step, parity, low - (step - 1)))
                if high + (step - 1) < count:
                    pairs.append((high, low))
                    arrivals[low].append((step, parity, high + (step - 1)))
            if pairs:
                plan[step, parity] = pairs
    return plan, arrivals


def lookup(values, index):
    value = jnp.int32(values[0])
    for i, v in enumerate(values[1:], 1):
        if v != values[0]:
            value = jnp.where(index == i, jnp.int32(v), value)
    return value


def spread(matrix, rows, cols, keep):
    size = matrix.shape[0]
    r = lax.broadcasted_iota(jnp.int32, (rows, size), 0)
    i = lax.broadcasted_iota(jnp.int32, (rows, size), 1)
    j = lax.broadcasted_iota(jnp.int32, (size, cols), 0)
    c = lax.broadcasted_iota(jnp.int32, (size, cols), 1)
    down = jnp.where(lax.rem(r, size) == i, 1.0, 0.0).astype(BF16)
    along = jnp.where(lax.rem(c, size) == j, 1.0, 0.0).astype(BF16)
    full = dot(dot(down, matrix.astype(BF16)).astype(BF16), along)
    block_row = lax.broadcasted_iota(jnp.int32, (rows, cols), 0) // size
    block_col = lax.broadcasted_iota(jnp.int32, (rows, cols), 1) // size
    return jnp.where(keep(block_row, block_col), full, 0.0).astype(BF16)


def prep_kernel(shape, here_ref, *refs):
    count, reps, base_rows, eigen_rows, fold = shape
    parts = refs[:count]
    w1_ref, but_ref, bu_ref, w5_ref, inv_ref, base3, eigen3, base, eigen, pad = refs[count:]
    z, rep = here_ref[0], here_ref[2]
    each = base_rows + eigen_rows
    for d in range(count):
        for e in range(reps):
            source = lax.rem(z + count - d, count) * reps + lax.rem(rep + reps - e, reps)
            base3[source] = parts[d][e * each : e * each + base_rows, :]
            eigen3[source] = parts[d][e * each + base_rows : (e + 1) * each, :]
    for s in range(count * reps):
        base[s * base_rows : (s + 1) * base_rows, :] = base3[s]
        eigen[s * eigen_rows : (s + 1) * eigen_rows, :] = eigen3[s]
    size = base.shape[0]
    basis = base[...]
    left, right = basis[:, :size], basis[:, size:]
    turned = basis.T
    left_t, right_t = turned[:size], turned[size:]
    wide = 2 * size * fold
    same = lambda r, c: r == c
    w1_ref[...] = spread(
        right, wide, wide, lambda r, c: (r // 2 == lax.rem(c, fold)) & (lax.rem(r, 2) == c // fold)
    )
    w5_ref[...] = spread(
        right_t, wide, wide, lambda r, c: (c // 2 == lax.rem(r, fold)) & (lax.rem(c, 2) == r // fold)
    )
    but_ref[...] = spread(left_t, GROUP * size, GROUP * size, same)
    bu_ref[...] = spread(left, GROUP * size, GROUP * size, same)
    values = eigen[...]
    inverse = 1.0 / (values + 0.1 * (jnp.sum(values) / (size * size)))
    shifted = pltpu.roll(inverse, size, 1)
    lane = lax.broadcasted_iota(jnp.int32, inverse.shape, 1)
    pad[pl.ds(0, size // 2, stride=2), :] = jnp.where(lane < size, inverse, shifted)
    pad[pl.ds(1, size // 2, stride=2), :] = jnp.where(lane < size, shifted, inverse)
    for g in range(GROUP):
        for h in range(fold // 2):
            inv_ref[g * size : (g + 1) * size, h * 2 * size : (h + 1) * 2 * size] = pad[...]


def rotation_constants(parts, here, reps, base_rows, eigen_rows, size, fold):
    count = len(parts)
    wide, tall = 2 * size * fold, GROUP * size
    shard = count * reps
    return call(
        functools.partial(prep_kernel, (count, reps, base_rows, eigen_rows, fold)),
        [
            jax.ShapeDtypeStruct((wide, wide), BF16),
            jax.ShapeDtypeStruct((tall, tall), BF16),
            jax.ShapeDtypeStruct((tall, tall), BF16),
            jax.ShapeDtypeStruct((wide, wide), BF16),
            jax.ShapeDtypeStruct((tall, size * fold), F32),
        ],
        [IN_SMEM] + [IN_VMEM] * count,
        [
            pltpu.VMEM((shard, base_rows, 2 * size), F32),
            pltpu.VMEM((shard, eigen_rows, 2 * size), F32),
            pltpu.VMEM((size, 2 * size), F32),
            pltpu.VMEM((size // 2, 2 * size), F32),
            pltpu.VMEM((size, 2 * size), F32),
        ],
        (here, *parts),
        flops=2 * wide * wide * 2 * size,
        grant=12 << 20,
    )


def rotate_kernel(sources, choice, splits, here_ref, *refs):
    inputs, refs = refs[:sources], refs[sources:]
    w1_ref, but_ref, bu_ref, w5_ref, inv_ref = refs[:5]
    outs = refs[5 : 6 + splits]
    tall = refs[6 + splits]
    scratch = refs[7 + splits :]
    first, second = scratch[: len(scratch) // 2], scratch[len(scratch) // 2 :]
    fold = inputs[0].shape[0] // TILE
    lanes = w1_ref.shape[0] // fold
    size = lanes // 2
    pairs = size // 2
    half = size * fold

    def gather_rows(q_ref):
        for a in range(pairs):
            for h in range(fold):
                tall[a * TILE : (a + 1) * TILE, h * lanes : (h + 1) * lanes] = q_ref[
                    h * TILE : (h + 1) * TILE, a * lanes : (a + 1) * lanes
                ]

    if sources == 1:
        gather_rows(inputs[0])
    else:
        which = lookup(choice, here_ref[0])
        for i in range(sources):
            pl.when(which == i)(functools.partial(gather_rows, inputs[i]))
    chunk = 8
    for a0 in range(0, pairs, chunk):
        rows = dot(tall[a0 * TILE : (a0 + chunk) * TILE, :], w1_ref[...])
        for a in range(a0, a0 + chunk):
            piece = rows[(a - a0) * TILE : (a - a0 + 1) * TILE]
            for c, ref in enumerate(first):
                low = c * lanes
                ref[pl.ds(2 * a, TILE, stride=size), :] = piece[:, low : low + lanes]
                ref[pl.ds(2 * a + 1, TILE, stride=size), :] = piece[:, half + low : half + low + lanes]
    but, bu, inverse = but_ref[...], bu_ref[...], inv_ref[...]
    step = GROUP * size
    for g in range(TILE // GROUP):
        part = jnp.concatenate([ref[g * step : (g + 1) * step, :].astype(BF16) for ref in first], axis=1)
        scaled = (dot(but, part) * inverse).astype(BF16)
        back = dot(bu, scaled)
        for c, ref in enumerate(second):
            ref[g * step : (g + 1) * step, :] = back[:, c * lanes : (c + 1) * lanes]
    for a in range(pairs):
        for odd in range(2):
            for c, ref in enumerate(second):
                low = odd * half + c * lanes
                tall[a * TILE : (a + 1) * TILE, low : low + lanes] = ref[
                    pl.ds(2 * a + odd, TILE, stride=size), :
                ].astype(BF16)
    for a0 in range(0, pairs, chunk):
        rows = dot(tall[a0 * TILE : (a0 + chunk) * TILE, :], w5_ref[...]).astype(BF16)
        for a in range(a0, a0 + chunk):
            for h in range(fold):
                value = rows[(a - a0) * TILE : (a - a0 + 1) * TILE, h * lanes : (h + 1) * lanes]
                outs[0][h * TILE : (h + 1) * TILE, a * lanes : (a + 1) * lanes] = value
                if splits:
                    per = fold // splits
                    low = (h % per) * TILE
                    outs[1 + h // per][low : low + TILE, a * lanes : (a + 1) * lanes] = value


def rotate(here, choice, inputs, constants, splits=0):
    rows, width = inputs[0].shape
    fold = rows // TILE
    wide = constants[0].shape[0]
    size = wide // (2 * fold)
    shapes = [jax.ShapeDtypeStruct((rows, width), BF16)]
    shapes += [jax.ShapeDtypeStruct((rows // splits, width), BF16)] * splits if splits else []
    return call(
        functools.partial(rotate_kernel, len(inputs), choice, splits),
        shapes,
        [IN_SMEM] + [IN_VMEM] * (len(inputs) + 5),
        [
            pltpu.VMEM((size // 2 * TILE, wide), BF16),
            *[pltpu.VMEM((TILE * size, 2 * size), F32)] * fold,
        ],
        (here, *inputs, *constants),
        flops=8 * rows * width * size * fold,
        grant=12 << 20,
    )


def fill(held, units, choices, here_ref):
    at = 0
    for candidates, choice in zip(units, choices):
        rows = candidates[0].shape[0]

        def take(ref, at=at, rows=rows):
            held[at : at + rows, :] = ref[...]

        if len(candidates) == 1:
            take(candidates[0])
        else:
            which = lookup(choice, here_ref[0])
            for i, ref in enumerate(candidates):
                pl.when(which == i)(functools.partial(take, ref))
        at += rows


def products(held, x_ref, kept_ref):
    total = x_ref.shape[0]
    step = min(256, total)
    for t in range(0, total, step):
        kept_ref[:, t : t + step] = lax.dot_general(
            x_ref[t : t + step, :], held[...], (((1,), (1,)), ((), ())), preferred_element_type=F32
        ).T


def grid_lookup(table, z, owner):
    value = lookup([row[0] for row in table], z)
    for o in range(1, len(table[0])):
        value = jnp.where(owner == o, lookup([row[o] for row in table], z), value)
    return value


def aligned(start, rows):
    return pl.ds(pl.multiple_of(start, rows), rows)


def early_kernel(shape, choices, table, piece, here_ref, *refs):
    refs = list(refs)
    units = [[refs.pop(0) for _ in range(n)] for n in shape]
    x_ref, kept_ref, *sent = refs[:-1]
    held = refs[-1]
    fill(held, units, choices, here_ref)
    products(held, x_ref, kept_ref)
    z, x = here_ref[0], here_ref[1]
    layers = len(sent) + 1
    for d, sent_ref in enumerate(sent, 1):
        target = lax.rem(x + d, layers)
        for p in range(len(table) - 1):
            start = grid_lookup(table[p], z, target)
            sent_ref[p * piece : (p + 1) * piece, :] = kept_ref[aligned(start, piece), :].astype(BF16)


def late_kernel(shape, choices, table, piece, here_ref, *refs):
    refs = list(refs)
    units = [[refs.pop(0) for _ in range(n)] for n in shape]
    x_ref, early_ref, kept_ref, *sent = refs[:-1]
    held = refs[-1]
    fill(held, units, choices, here_ref)
    products(held, x_ref, kept_ref)
    z, x = here_ref[0], here_ref[1]
    layers = len(sent) + 1
    for d, sent_ref in enumerate(sent, 1):
        start = grid_lookup(table[-1], z, lax.rem(x + d, layers))
        last = early_ref.shape[0]

        @pl.when(start == last)
        def _(sent_ref=sent_ref):
            sent_ref[...] = kept_ref[...].astype(BF16)

        @pl.when(start != last)
        def _(sent_ref=sent_ref, start=start):
            sent_ref[...] = early_ref[aligned(start, piece), :].astype(BF16)


def finish_kernel(table, places, piece, layers, here_ref, early_ref, late_ref, *refs):
    *received, out_ref = refs
    z, x = here_ref[0], here_ref[1]
    shifts = layers - 1
    first, second = received[:shifts], received[shifts:]
    last = early_ref.shape[0]
    count = len(table)
    for p in range(count):
        start = grid_lookup(table[p], z, x)
        place = aligned(grid_lookup(places[p], z, x), piece)
        if p < count - 1:
            value = early_ref[aligned(start, piece), :]
            for ref in first:
                value = value + ref[p * piece : (p + 1) * piece, :].astype(F32)
            out_ref[place, :] = value
            continue
        other = second[0][...].astype(F32)
        for ref in second[1:]:
            other = other + ref[...].astype(F32)

        @pl.when(start == last)
        def _():
            out_ref[place, :] = late_ref[...] + other

        @pl.when(start != last)
        def _():
            out_ref[place, :] = early_ref[aligned(start, piece), :] + other


def load_kernel(x_ref, out_ref, sem):
    pieces = sem.shape[0]
    step = x_ref.shape[0] // pieces
    copies = []
    for i in range(pieces):
        rows = pl.ds(i * step, step)
        copies.append(pltpu.make_async_copy(x_ref.at[rows], out_ref.at[rows], sem.at[i]))
    for copy in copies:
        copy.start()
    for copy in copies:
        copy.wait()


def resident(x):
    return pl.pallas_call(
        load_kernel,
        out_shape=pltpu.VMEM(x.shape, x.dtype),
        in_specs=[pl.BlockSpec(memory_space=pltpu.HBM)],
        out_specs=IN_VMEM,
        scratch_shapes=[pltpu.SemaphoreType.DMA((8,))],
        compiler_params=pltpu.CompilerParams(vmem_limit_bytes=12 << 20),
        cost_estimate=pl.CostEstimate(
            flops=0, bytes_accessed=2 * x.size * x.dtype.itemsize, transcendentals=0
        ),
    )(x)


def body(train_grads, queries, bases, eigenvalues):
    blocks, layers, reps = lax.axis_size("blk"), lax.axis_size("layer"), lax.axis_size("rep")
    z, x, rep = lax.axis_index("blk"), lax.axis_index("layer"), lax.axis_index("rep")
    train = train_grads[0]
    own = queries[0, 0]
    base_rows, lanes = bases.shape[1:]
    size = lanes // 2
    rows = own.shape[0]
    fold = rows // TILE
    per_owner = blocks // layers

    plan, arrivals = line_plan(blocks)
    here = jnp.stack([z, x, rep]).astype(jnp.int32)
    splits = 2

    raw, turned = {}, {}
    raw[1, 1] = lax.ppermute(own, "blk", plan[1, 1])
    raw[1, 0] = lax.ppermute(own, "blk", plan[1, 0])

    eigen = eigenvalues.reshape(-1, lanes)
    eigen_rows = eigen.shape[0]
    packed = jnp.concatenate([bases[0].astype(F32), eigen], axis=0)
    pair = [packed]
    for e in range(1, reps):
        pair.append(lax.ppermute(packed, "rep", [(r, (r + e) % reps) for r in range(reps)]))
    pair = jnp.concatenate(pair, axis=0)
    parts = [pair]
    for d in range(1, blocks):
        parts.append(lax.ppermute(pair, "blk", [(a, (a + d) % blocks) for a in range(blocks)]))
    train, _ = lax.optimization_barrier((train, pair))
    train = resident(train)
    raw[1, 1], train = lax.optimization_barrier((raw[1, 1], train))
    raw[2, 0] = lax.ppermute(raw[1, 1], "blk", plan[2, 0])

    constants = rotation_constants(parts, here, reps, base_rows, eigen_rows, size, fold)
    alone = [0] * blocks
    whole_first, *turned[1, 0] = rotate(here, alone, [raw[1, 0]], constants, splits)
    whole_own, = rotate(here, alone, [own], constants)

    block_of = [list(range(blocks))] + [[a[j][2] for a in arrivals] for j in range(blocks - 1)]
    source_of = [None] + [[a[j][:2] for a in arrivals] for j in range(blocks - 1)]
    units, choices = [[whole_own], [whole_first]], [alone, alone]
    gate = whole_own
    for step, parity in plan:
        if step == 1 or (step, parity) in raw:
            continue
        before = (step - 1, 1 - parity)
        if before not in turned:
            turned[before] = rotate(here, alone, [raw[before]], constants, splits)[1:]
        pieces = turned[before]
        if step > 2:
            pieces = [lax.optimization_barrier((w, gate))[0] for w in pieces]
        turned[step, parity] = [lax.ppermute(w, "blk", plan[step, parity]) for w in pieces]

    for j in range(2, blocks):
        names = sorted(set(source_of[j]))
        fresh = [n for n in names if n in raw and n not in turned]
        ready = [n for n in names if n not in fresh]
        if fresh:
            choice = [fresh.index(s) if s in fresh else 0 for s in source_of[j]]
            wide = rotate(here, choice, [raw[n] for n in fresh], constants, splits if ready else 0)
        if not ready:
            units.append([wide[0]])
            choices.append(alone)
            continue
        for part in range(splits):
            candidates = [wide[1 + part]] if fresh else []
            offset = len(candidates)
            candidates += [turned[n][part] for n in ready]
            units.append(candidates)
            choices.append([0 if s in fresh else offset + ready.index(s) for s in source_of[j]])

    piece = rows // splits
    count = per_owner * splits
    table = [[[0] * layers for _ in range(blocks)] for _ in range(count)]
    places = [[[0] * layers for _ in range(blocks)] for _ in range(count)]
    for a in range(blocks):
        for o in range(layers):
            mine = [j for j in range(blocks) if block_of[j][a] // per_owner == o]
            for p in range(count):
                j, part = mine[p // splits], p % splits
                table[p][a][o] = j * rows + part * piece
                places[p][a][o] = block_of[j][a] % per_owner * rows + part * piece

    def shifted(sent):
        return [
            lax.ppermute(s, "layer", [(o, (o + d) % layers) for o in range(layers)])
            for d, s in enumerate(sent, 1)
        ]

    def scores(kernel, units, choices, inputs, sent_rows, grant):
        held = sum(u[0].shape[0] for u in units)
        total, width = train.shape
        flat = [w for u in units for w in u] + [train] + inputs
        sent_shape = jax.ShapeDtypeStruct((sent_rows, total), BF16)
        return call(
            functools.partial(kernel, [len(u) for u in units], choices, table, piece),
            [jax.ShapeDtypeStruct((held, total), F32)] + [sent_shape] * (layers - 1),
            [IN_SMEM] + [IN_VMEM] * len(flat),
            [pltpu.VMEM((held, width), BF16)],
            (here, *flat),
            flops=2 * held * total * width,
            grant=grant,
        )

    early, *sent = scores(early_kernel, units[:-1], choices[:-1], [], (count - 1) * piece, 16 << 20)
    first = shifted(sent)
    late, *sent = scores(late_kernel, units[-1:], choices[-1:], [early], piece, 12 << 20)
    second = shifted(sent)
    out = call(
        functools.partial(finish_kernel, table, places, piece, layers),
        jax.ShapeDtypeStruct((per_owner * rows, train.shape[0]), F32),
        [IN_SMEM] + [IN_VMEM] * (2 + 2 * (layers - 1)),
        [],
        (here, early, late, *first, *second),
        flops=per_owner * rows * train.shape[0],
        grant=12 << 20,
    )
    return out[None]


def solution(mesh):
    return jax.shard_map(
        body,
        mesh=mesh,
        in_specs=(
            P("layer", ("groups", "blk"), None),
            P("layer", "rep", ("groups", "blk"), None),
            P("layer", ("blk", "rep"), None),
            P("layer", ("blk", "rep")),
        ),
        out_specs=P("rep", "layer", ("groups", "blk")),
        check_vma=False,
    )
```

```python
import functools

import jax
import jax.numpy as jnp
from jax import lax
from jax.experimental import pallas as pl
from jax.experimental.pallas import tpu as pltpu
from jax.sharding import PartitionSpec as P

TILE = 16
HALF = 8
BF16, F32 = jnp.bfloat16, jnp.float32
IN_VMEM = pl.BlockSpec(memory_space=pltpu.VMEM)
IN_SMEM = pl.BlockSpec(memory_space=pltpu.SMEM)


def dot(a, b):
    return jnp.dot(a, b, preferred_element_type=F32)


def call(kernel, out_shape, in_specs, scratch, args, flops, grant):
    outs = out_shape if isinstance(out_shape, (list, tuple)) else [out_shape]
    moved = sum(a.size * a.dtype.itemsize for a in list(args) + list(outs))
    return pl.pallas_call(
        kernel,
        out_shape=out_shape,
        in_specs=in_specs,
        out_specs=jax.tree.map(lambda _: IN_VMEM, out_shape),
        scratch_shapes=scratch,
        compiler_params=pltpu.CompilerParams(vmem_limit_bytes=grant),
        cost_estimate=pl.CostEstimate(flops=flops, bytes_accessed=moved, transcendentals=0),
    )(*args)


def line_plan(count):
    plan, arrivals = {}, [[] for _ in range(count)]
    for step in range(1, count):
        for parity in range(2):
            pairs = []
            for low in range(parity, count - 1, 2):
                high = low + 1
                if low - (step - 1) >= 0:
                    pairs.append((low, high))
                    arrivals[high].append((step, parity, low - (step - 1)))
                if high + (step - 1) < count:
                    pairs.append((high, low))
                    arrivals[low].append((step, parity, high + (step - 1)))
            if pairs:
                plan[step, parity] = pairs
    return plan, arrivals


def lookup(values, index):
    value = jnp.int32(values[0])
    for i, v in enumerate(values[1:], 1):
        if v != values[0]:
            value = jnp.where(index == i, jnp.int32(v), value)
    return value


def spread(matrix, rows, cols, keep):
    size = matrix.shape[0]
    r = lax.broadcasted_iota(jnp.int32, (rows, size), 0)
    i = lax.broadcasted_iota(jnp.int32, (rows, size), 1)
    j = lax.broadcasted_iota(jnp.int32, (size, cols), 0)
    c = lax.broadcasted_iota(jnp.int32, (size, cols), 1)
    down = jnp.where(lax.rem(r, size) == i, 1.0, 0.0).astype(BF16)
    along = jnp.where(lax.rem(c, size) == j, 1.0, 0.0).astype(BF16)
    full = dot(dot(down, matrix.astype(BF16)).astype(BF16), along)
    block_row = lax.broadcasted_iota(jnp.int32, (rows, cols), 0) // size
    block_col = lax.broadcasted_iota(jnp.int32, (rows, cols), 1) // size
    return jnp.where(keep(block_row, block_col), full, 0.0).astype(BF16)


def comb(matrix, out_ref):
    size = matrix.shape[0]
    wide = size * HALF
    j = lax.broadcasted_iota(jnp.int32, (size, wide), 0)
    c = lax.broadcasted_iota(jnp.int32, (size, wide), 1)
    rows = dot(matrix.astype(BF16), jnp.where(c // HALF == j, 1.0, 0.0).astype(BF16))
    r = lax.broadcasted_iota(jnp.int32, (HALF, wide), 0)
    c = lax.broadcasted_iota(jnp.int32, (HALF, wide), 1)
    keep = r == lax.rem(c, HALF)
    for i in range(0, size, 2):
        pair = [
            jnp.where(keep, jnp.broadcast_to(rows[k : k + 1], (HALF, wide)), 0.0) for k in (i, i + 1)
        ]
        out_ref[i * HALF : (i + 2) * HALF, :] = jnp.concatenate(pair, axis=0).astype(BF16)


def prep_kernel(shape, here_ref, *refs):
    count, reps, base_rows, eigen_rows, fold = shape
    parts = refs[:count]
    w1_ref, but_ref, bu_ref, w5_ref, inv_ref, base3, eigen3, base, eigen, pad = refs[count:]
    z, rep = here_ref[0], here_ref[2]
    each = base_rows + eigen_rows
    for d in range(count):
        for e in range(reps):
            source = lax.rem(z + count - d, count) * reps + lax.rem(rep + reps - e, reps)
            base3[source] = parts[d][e * each : e * each + base_rows, :]
            eigen3[source] = parts[d][e * each + base_rows : (e + 1) * each, :]
    for s in range(count * reps):
        base[s * base_rows : (s + 1) * base_rows, :] = base3[s]
        eigen[s * eigen_rows : (s + 1) * eigen_rows, :] = eigen3[s]
    size = base.shape[0]
    basis = base[...]
    left, right = basis[:, :size], basis[:, size:]
    turned = basis.T
    left_t, right_t = turned[:size], turned[size:]
    wide = 2 * size * fold
    w1_ref[...] = spread(
        right, wide, wide, lambda r, c: (r // 2 == lax.rem(c, fold)) & (lax.rem(r, 2) == c // fold)
    )
    w5_ref[...] = spread(
        right_t, wide, wide, lambda r, c: (c // 2 == lax.rem(r, fold)) & (lax.rem(c, 2) == r // fold)
    )
    comb(left_t, but_ref)
    comb(left, bu_ref)
    values = eigen[...]
    inverse = 1.0 / (values + 0.1 * (jnp.sum(values) / (size * size)))
    shifted = pltpu.roll(inverse, size, 1)
    lane = lax.broadcasted_iota(jnp.int32, inverse.shape, 1)
    pad[pl.ds(0, size // 2, stride=2), :] = jnp.where(lane < size, inverse, shifted)
    pad[pl.ds(1, size // 2, stride=2), :] = jnp.where(lane < size, shifted, inverse)
    for i in range(size):
        row = jnp.broadcast_to(pad[i : i + 1, :], (HALF, 2 * size))
        for h in range(fold // 2):
            inv_ref[i * HALF : (i + 1) * HALF, h * 2 * size : (h + 1) * 2 * size] = row


def rotation_constants(parts, here, reps, base_rows, eigen_rows, size, fold):
    count = len(parts)
    wide, tall = 2 * size * fold, HALF * size
    shard = count * reps
    return call(
        functools.partial(prep_kernel, (count, reps, base_rows, eigen_rows, fold)),
        [
            jax.ShapeDtypeStruct((wide, wide), BF16),
            jax.ShapeDtypeStruct((tall, tall), BF16),
            jax.ShapeDtypeStruct((tall, tall), BF16),
            jax.ShapeDtypeStruct((wide, wide), BF16),
            jax.ShapeDtypeStruct((tall, size * fold), F32),
        ],
        [IN_SMEM] + [IN_VMEM] * count,
        [
            pltpu.VMEM((shard, base_rows, 2 * size), F32),
            pltpu.VMEM((shard, eigen_rows, 2 * size), F32),
            pltpu.VMEM((size, 2 * size), F32),
            pltpu.VMEM((size // 2, 2 * size), F32),
            pltpu.VMEM((size, 2 * size), F32),
        ],
        (here, *parts),
        flops=2 * wide * wide * 2 * size,
        grant=12 << 20,
    )


def rotate_kernel(sources, choice, splits, here_ref, *refs):
    inputs, refs = refs[:sources], refs[sources:]
    w1_ref, but_ref, bu_ref, w5_ref, inv_ref = refs[:5]
    outs = refs[5 : 6 + splits]
    tall, first, second = refs[6 + splits :]
    fold = inputs[0].shape[0] // TILE
    lanes = w1_ref.shape[0] // fold
    size = lanes // 2
    pairs = size // 2
    half = size * fold

    def gather_rows(q_ref):
        for a in range(pairs):
            for h in range(fold):
                tall[a * TILE : (a + 1) * TILE, h * lanes : (h + 1) * lanes] = q_ref[
                    h * TILE : (h + 1) * TILE, a * lanes : (a + 1) * lanes
                ]

    if sources == 1:
        gather_rows(inputs[0])
    else:
        which = lookup(choice, here_ref[0])
        for i in range(sources):
            pl.when(which == i)(functools.partial(gather_rows, inputs[i]))
    chunk = 8
    parts = TILE // HALF
    for a0 in range(0, pairs, chunk):
        rows = dot(tall[a0 * TILE : (a0 + chunk) * TILE, :], w1_ref[...])
        for a in range(a0, a0 + chunk):
            for part in range(parts):
                low = (a - a0) * TILE + part * HALF
                for odd in range(2):
                    at = (2 * a + odd) * HALF
                    first[part, at : at + HALF, :] = rows[low : low + HALF, odd * half : (odd + 1) * half]
    but, bu, inverse = but_ref[...], bu_ref[...], inv_ref[...]
    for part in range(parts):
        scaled = (dot(but, first[part].astype(BF16)) * inverse).astype(BF16)
        second[part] = dot(bu, scaled)
    for a in range(pairs):
        for odd in range(2):
            at = (2 * a + odd) * HALF
            value = jnp.concatenate([second[part, at : at + HALF, :] for part in range(parts)], axis=0)
            tall[a * TILE : (a + 1) * TILE, odd * half : (odd + 1) * half] = value.astype(BF16)
    for a0 in range(0, pairs, chunk):
        rows = dot(tall[a0 * TILE : (a0 + chunk) * TILE, :], w5_ref[...]).astype(BF16)
        for a in range(a0, a0 + chunk):
            for h in range(fold):
                value = rows[(a - a0) * TILE : (a - a0 + 1) * TILE, h * lanes : (h + 1) * lanes]
                outs[0][h * TILE : (h + 1) * TILE, a * lanes : (a + 1) * lanes] = value
                if splits:
                    per = fold // splits
                    low = (h % per) * TILE
                    outs[1 + h // per][low : low + TILE, a * lanes : (a + 1) * lanes] = value


def rotate(here, choice, inputs, constants, splits=0):
    rows, width = inputs[0].shape
    fold = rows // TILE
    wide = constants[0].shape[0]
    size = wide // (2 * fold)
    shapes = [jax.ShapeDtypeStruct((rows, width), BF16)]
    shapes += [jax.ShapeDtypeStruct((rows // splits, width), BF16)] * splits if splits else []
    return call(
        functools.partial(rotate_kernel, len(inputs), choice, splits),
        shapes,
        [IN_SMEM] + [IN_VMEM] * (len(inputs) + 5),
        [
            pltpu.VMEM((size // 2 * TILE, wide), BF16),
            pltpu.VMEM((TILE // HALF, size * HALF, size * fold), F32),
            pltpu.VMEM((TILE // HALF, size * HALF, size * fold), F32),
        ],
        (here, *inputs, *constants),
        flops=8 * rows * width * size * fold,
        grant=12 << 20,
    )


def fill(held, units, choices, here_ref):
    at = 0
    for candidates, choice in zip(units, choices):
        rows = candidates[0].shape[0]

        def take(ref, at=at, rows=rows):
            held[at : at + rows, :] = ref[...]

        if len(candidates) == 1:
            take(candidates[0])
        else:
            which = lookup(choice, here_ref[0])
            for i, ref in enumerate(candidates):
                pl.when(which == i)(functools.partial(take, ref))
        at += rows


def products(held, x_ref, kept_ref):
    total = x_ref.shape[0]
    step = min(256, total)
    for t in range(0, total, step):
        kept_ref[:, t : t + step] = lax.dot_general(
            x_ref[t : t + step, :], held[...], (((1,), (1,)), ((), ())), preferred_element_type=F32
        ).T


def grid_lookup(table, z, owner):
    value = lookup([row[0] for row in table], z)
    for o in range(1, len(table[0])):
        value = jnp.where(owner == o, lookup([row[o] for row in table], z), value)
    return value


def aligned(start, rows):
    return pl.ds(pl.multiple_of(start, rows), rows)


def early_kernel(shape, choices, table, piece, here_ref, *refs):
    refs = list(refs)
    units = [[refs.pop(0) for _ in range(n)] for n in shape]
    x_ref, kept_ref, *sent = refs[:-1]
    held = refs[-1]
    fill(held, units, choices, here_ref)
    products(held, x_ref, kept_ref)
    z, x = here_ref[0], here_ref[1]
    layers = len(sent) + 1
    for d, sent_ref in enumerate(sent, 1):
        target = lax.rem(x + d, layers)
        for p in range(len(table) - 1):
            start = grid_lookup(table[p], z, target)
            sent_ref[p * piece : (p + 1) * piece, :] = kept_ref[aligned(start, piece), :].astype(BF16)


def late_kernel(shape, choices, table, piece, here_ref, *refs):
    refs = list(refs)
    units = [[refs.pop(0) for _ in range(n)] for n in shape]
    x_ref, early_ref, kept_ref, *sent = refs[:-1]
    held = refs[-1]
    fill(held, units, choices, here_ref)
    products(held, x_ref, kept_ref)
    z, x = here_ref[0], here_ref[1]
    layers = len(sent) + 1
    for d, sent_ref in enumerate(sent, 1):
        start = grid_lookup(table[-1], z, lax.rem(x + d, layers))
        last = early_ref.shape[0]

        @pl.when(start == last)
        def _(sent_ref=sent_ref):
            sent_ref[...] = kept_ref[...].astype(BF16)

        @pl.when(start != last)
        def _(sent_ref=sent_ref, start=start):
            sent_ref[...] = early_ref[aligned(start, piece), :].astype(BF16)


def finish_kernel(table, places, piece, layers, here_ref, early_ref, late_ref, *refs):
    *received, out_ref = refs
    z, x = here_ref[0], here_ref[1]
    shifts = layers - 1
    first, second = received[:shifts], received[shifts:]
    last = early_ref.shape[0]
    count = len(table)
    for p in range(count):
        start = grid_lookup(table[p], z, x)
        place = aligned(grid_lookup(places[p], z, x), piece)
        if p < count - 1:
            value = early_ref[aligned(start, piece), :]
            for ref in first:
                value = value + ref[p * piece : (p + 1) * piece, :].astype(F32)
            out_ref[place, :] = value
            continue
        other = second[0][...].astype(F32)
        for ref in second[1:]:
            other = other + ref[...].astype(F32)

        @pl.when(start == last)
        def _():
            out_ref[place, :] = late_ref[...] + other

        @pl.when(start != last)
        def _():
            out_ref[place, :] = early_ref[aligned(start, piece), :] + other


def load_kernel(x_ref, out_ref, sem):
    pieces = sem.shape[0]
    step = x_ref.shape[0] // pieces
    copies = []
    for i in range(pieces):
        rows = pl.ds(i * step, step)
        copies.append(pltpu.make_async_copy(x_ref.at[rows], out_ref.at[rows], sem.at[i]))
    for copy in copies:
        copy.start()
    for copy in copies:
        copy.wait()


def resident(x):
    return pl.pallas_call(
        load_kernel,
        out_shape=pltpu.VMEM(x.shape, x.dtype),
        in_specs=[pl.BlockSpec(memory_space=pltpu.HBM)],
        out_specs=IN_VMEM,
        scratch_shapes=[pltpu.SemaphoreType.DMA((8,))],
        compiler_params=pltpu.CompilerParams(vmem_limit_bytes=12 << 20),
        cost_estimate=pl.CostEstimate(
            flops=0, bytes_accessed=2 * x.size * x.dtype.itemsize, transcendentals=0
        ),
    )(x)


def steps(train_grads, queries, bases, eigenvalues):
    blocks, layers, reps = lax.axis_size("blk"), lax.axis_size("layer"), lax.axis_size("rep")
    z, x, rep = lax.axis_index("blk"), lax.axis_index("layer"), lax.axis_index("rep")
    train = train_grads[0]
    own = queries[0, 0]
    base_rows, lanes = bases.shape[1:]
    size = lanes // 2
    rows = own.shape[0]
    fold = rows // TILE
    per_owner = blocks // layers

    plan, arrivals = line_plan(blocks)
    here = jnp.stack([z, x, rep]).astype(jnp.int32)
    splits = 2

    raw, turned = {}, {}
    raw[1, 1] = lax.ppermute(own, "blk", plan[1, 1])
    raw[1, 0] = lax.ppermute(own, "blk", plan[1, 0])

    eigen = eigenvalues.reshape(-1, lanes)
    eigen_rows = eigen.shape[0]
    packed = jnp.concatenate([bases[0].astype(F32), eigen], axis=0)
    pair = [packed]
    for e in range(1, reps):
        pair.append(lax.ppermute(packed, "rep", [(r, (r + e) % reps) for r in range(reps)]))
    pair = jnp.concatenate(pair, axis=0)
    parts = [pair]
    for d in range(1, blocks):
        parts.append(lax.ppermute(pair, "blk", [(a, (a + d) % blocks) for a in range(blocks)]))
    train, _ = lax.optimization_barrier((train, pair))
    train = resident(train)
    raw[1, 1], train = lax.optimization_barrier((raw[1, 1], train))
    raw[2, 0] = lax.ppermute(raw[1, 1], "blk", plan[2, 0])

    constants = rotation_constants(parts, here, reps, base_rows, eigen_rows, size, fold)
    alone = [0] * blocks
    whole_first, *turned[1, 0] = rotate(here, alone, [raw[1, 0]], constants, splits)
    whole_own, = rotate(here, alone, [own], constants)

    block_of = [list(range(blocks))] + [[a[j][2] for a in arrivals] for j in range(blocks - 1)]
    source_of = [None] + [[a[j][:2] for a in arrivals] for j in range(blocks - 1)]
    units, choices = [[whole_own], [whole_first]], [alone, alone]
    gate = whole_own
    for step, parity in plan:
        if step == 1 or (step, parity) in raw:
            continue
        before = (step - 1, 1 - parity)
        if before not in turned:
            turned[before] = rotate(here, alone, [raw[before]], constants, splits)[1:]
        pieces = turned[before]
        if step > 2:
            pieces = [lax.optimization_barrier((w, gate))[0] for w in pieces]
        turned[step, parity] = [lax.ppermute(w, "blk", plan[step, parity]) for w in pieces]

    for j in range(2, blocks):
        names = sorted(set(source_of[j]))
        fresh = [n for n in names if n in raw and n not in turned]
        ready = [n for n in names if n not in fresh]
        if fresh:
            choice = [fresh.index(s) if s in fresh else 0 for s in source_of[j]]
            wide = rotate(here, choice, [raw[n] for n in fresh], constants, splits if ready else 0)
        if not ready:
            units.append([wide[0]])
            choices.append(alone)
            continue
        for part in range(splits):
            candidates = [wide[1 + part]] if fresh else []
            offset = len(candidates)
            candidates += [turned[n][part] for n in ready]
            units.append(candidates)
            choices.append([0 if s in fresh else offset + ready.index(s) for s in source_of[j]])

    piece = rows // splits
    count = per_owner * splits
    table = [[[0] * layers for _ in range(blocks)] for _ in range(count)]
    places = [[[0] * layers for _ in range(blocks)] for _ in range(count)]
    for a in range(blocks):
        for o in range(layers):
            mine = [j for j in range(blocks) if block_of[j][a] // per_owner == o]
            for p in range(count):
                j, part = mine[p // splits], p % splits
                table[p][a][o] = j * rows + part * piece
                places[p][a][o] = block_of[j][a] % per_owner * rows + part * piece

    def shifted(sent):
        return [
            lax.ppermute(s, "layer", [(o, (o + d) % layers) for o in range(layers)])
            for d, s in enumerate(sent, 1)
        ]

    def scores(kernel, units, choices, inputs, sent_rows, grant):
        held = sum(u[0].shape[0] for u in units)
        total, width = train.shape
        flat = [w for u in units for w in u] + [train] + inputs
        sent_shape = jax.ShapeDtypeStruct((sent_rows, total), BF16)
        return call(
            functools.partial(kernel, [len(u) for u in units], choices, table, piece),
            [jax.ShapeDtypeStruct((held, total), F32)] + [sent_shape] * (layers - 1),
            [IN_SMEM] + [IN_VMEM] * len(flat),
            [pltpu.VMEM((held, width), BF16)],
            (here, *flat),
            flops=2 * held * total * width,
            grant=grant,
        )

    early, *sent = scores(early_kernel, units[:-1], choices[:-1], [], (count - 1) * piece, 16 << 20)
    first = shifted(sent)
    late, *sent = scores(late_kernel, units[-1:], choices[-1:], [early], piece, 12 << 20)
    second = shifted(sent)
    out = call(
        functools.partial(finish_kernel, table, places, piece, layers),
        jax.ShapeDtypeStruct((per_owner * rows, train.shape[0]), F32),
        [IN_SMEM] + [IN_VMEM] * (2 + 2 * (layers - 1)),
        [],
        (here, early, late, *first, *second),
        flops=per_owner * rows * train.shape[0],
        grant=12 << 20,
    )
    return out[None]


def solution(mesh):
    return jax.shard_map(
        steps,
        mesh=mesh,
        in_specs=(
            P("layer", ("groups", "blk"), None),
            P("layer", "rep", ("groups", "blk"), None),
            P("layer", ("blk", "rep"), None),
            P("layer", ("blk", "rep")),
        ),
        out_specs=P("rep", "layer", ("groups", "blk")),
        check_vma=False,
    )
```

```python
import functools

import jax
import jax.numpy as jnp
from jax import lax
from jax.experimental import pallas as pl
from jax.experimental.pallas import tpu as pltpu
from jax.sharding import PartitionSpec as P

TILE = 16
HALF = 8
BF16, F32 = jnp.bfloat16, jnp.float32
IN_VMEM = pl.BlockSpec(memory_space=pltpu.VMEM)
IN_SMEM = pl.BlockSpec(memory_space=pltpu.SMEM)


def dot(a, b):
    return jnp.dot(a, b, preferred_element_type=F32)


def call(kernel, out_shape, in_specs, scratch, args, flops, grant):
    outs = out_shape if isinstance(out_shape, (list, tuple)) else [out_shape]
    moved = sum(a.size * a.dtype.itemsize for a in list(args) + list(outs))
    return pl.pallas_call(
        kernel,
        out_shape=out_shape,
        in_specs=in_specs,
        out_specs=jax.tree.map(lambda _: IN_VMEM, out_shape),
        scratch_shapes=scratch,
        compiler_params=pltpu.CompilerParams(vmem_limit_bytes=grant),
        cost_estimate=pl.CostEstimate(flops=flops, bytes_accessed=moved, transcendentals=0),
    )(*args)


def line_plan(count):
    plan, arrivals = {}, [[] for _ in range(count)]
    for step in range(1, count):
        for parity in range(2):
            pairs = []
            for low in range(parity, count - 1, 2):
                high = low + 1
                if low - (step - 1) >= 0:
                    pairs.append((low, high))
                    arrivals[high].append((step, parity, low - (step - 1)))
                if high + (step - 1) < count:
                    pairs.append((high, low))
                    arrivals[low].append((step, parity, high + (step - 1)))
            if pairs:
                plan[step, parity] = pairs
    return plan, arrivals


def lookup(values, index):
    value = jnp.int32(values[0])
    for i, v in enumerate(values[1:], 1):
        if v != values[0]:
            value = jnp.where(index == i, jnp.int32(v), value)
    return value


def spread(matrix, rows, cols, keep):
    size = matrix.shape[0]
    r = lax.broadcasted_iota(jnp.int32, (rows, size), 0)
    i = lax.broadcasted_iota(jnp.int32, (rows, size), 1)
    j = lax.broadcasted_iota(jnp.int32, (size, cols), 0)
    c = lax.broadcasted_iota(jnp.int32, (size, cols), 1)
    down = jnp.where(lax.rem(r, size) == i, 1.0, 0.0).astype(BF16)
    along = jnp.where(lax.rem(c, size) == j, 1.0, 0.0).astype(BF16)
    full = dot(dot(down, matrix.astype(BF16)).astype(BF16), along)
    block_row = lax.broadcasted_iota(jnp.int32, (rows, cols), 0) // size
    block_col = lax.broadcasted_iota(jnp.int32, (rows, cols), 1) // size
    return jnp.where(keep(block_row, block_col), full, 0.0).astype(BF16)


def comb(matrix, out_ref):
    size = matrix.shape[0]
    wide = size * HALF
    j = lax.broadcasted_iota(jnp.int32, (size, wide), 0)
    c = lax.broadcasted_iota(jnp.int32, (size, wide), 1)
    rows = dot(matrix.astype(BF16), jnp.where(c // HALF == j, 1.0, 0.0).astype(BF16))
    r = lax.broadcasted_iota(jnp.int32, (HALF, wide), 0)
    c = lax.broadcasted_iota(jnp.int32, (HALF, wide), 1)
    keep = r == lax.rem(c, HALF)
    for i in range(0, size, 2):
        pair = [
            jnp.where(keep, jnp.broadcast_to(rows[k : k + 1], (HALF, wide)), 0.0) for k in (i, i + 1)
        ]
        out_ref[i * HALF : (i + 2) * HALF, :] = jnp.concatenate(pair, axis=0).astype(BF16)


def prep_kernel(shape, here_ref, *refs):
    count, reps, base_rows, eigen_rows, fold = shape
    parts = refs[:count]
    w1_ref, but_ref, bu_ref, w5_ref, inv_ref, base3, eigen3, base, eigen, pad = refs[count:]
    z, rep = here_ref[0], here_ref[2]
    each = base_rows + eigen_rows
    for d in range(count):
        for e in range(reps):
            source = lax.rem(z + count - d, count) * reps + lax.rem(rep + reps - e, reps)
            base3[source] = parts[d][e * each : e * each + base_rows, :]
            eigen3[source] = parts[d][e * each + base_rows : (e + 1) * each, :]
    for s in range(count * reps):
        base[s * base_rows : (s + 1) * base_rows, :] = base3[s]
        eigen[s * eigen_rows : (s + 1) * eigen_rows, :] = eigen3[s]
    size = base.shape[0]
    basis = base[...]
    left, right = basis[:, :size], basis[:, size:]
    turned = basis.T
    left_t, right_t = turned[:size], turned[size:]
    wide = 2 * size * fold
    w1_ref[...] = spread(
        right, wide, wide, lambda r, c: (r // 2 == lax.rem(c, fold)) & (lax.rem(r, 2) == c // fold)
    )
    w5_ref[...] = spread(
        right_t, wide, wide, lambda r, c: (c // 2 == lax.rem(r, fold)) & (lax.rem(c, 2) == r // fold)
    )
    comb(left_t, but_ref)
    comb(left, bu_ref)
    values = eigen[...]
    inverse = 1.0 / (values + 0.1 * (jnp.sum(values) / (size * size)))
    shifted = pltpu.roll(inverse, size, 1)
    lane = lax.broadcasted_iota(jnp.int32, inverse.shape, 1)
    pad[pl.ds(0, size // 2, stride=2), :] = jnp.where(lane < size, inverse, shifted)
    pad[pl.ds(1, size // 2, stride=2), :] = jnp.where(lane < size, shifted, inverse)
    for i in range(size):
        row = jnp.broadcast_to(pad[i : i + 1, :], (HALF, 2 * size))
        for h in range(fold // 2):
            inv_ref[i * HALF : (i + 1) * HALF, h * 2 * size : (h + 1) * 2 * size] = row


def rotation_constants(parts, here, reps, base_rows, eigen_rows, size, fold):
    count = len(parts)
    wide, tall = 2 * size * fold, HALF * size
    shard = count * reps
    return call(
        functools.partial(prep_kernel, (count, reps, base_rows, eigen_rows, fold)),
        [
            jax.ShapeDtypeStruct((wide, wide), BF16),
            jax.ShapeDtypeStruct((tall, tall), BF16),
            jax.ShapeDtypeStruct((tall, tall), BF16),
            jax.ShapeDtypeStruct((wide, wide), BF16),
            jax.ShapeDtypeStruct((tall, size * fold), F32),
        ],
        [IN_SMEM] + [IN_VMEM] * count,
        [
            pltpu.VMEM((shard, base_rows, 2 * size), F32),
            pltpu.VMEM((shard, eigen_rows, 2 * size), F32),
            pltpu.VMEM((size, 2 * size), F32),
            pltpu.VMEM((size // 2, 2 * size), F32),
            pltpu.VMEM((size, 2 * size), F32),
        ],
        (here, *parts),
        flops=2 * wide * wide * 2 * size,
        grant=12 << 20,
    )


def pack_kernel(bases_ref, eigen_ref, out_ref):
    rows = bases_ref.shape[0]
    out_ref[:rows, :] = bases_ref[...].astype(F32)
    out_ref[rows:, :] = eigen_ref[...]


def head_kernel(rows_ref, out_ref):
    out_ref[...] = rows_ref[: out_ref.shape[0], :]


def head(value, rows):
    shape = jax.ShapeDtypeStruct((rows, value.shape[1]), value.dtype)
    return call(head_kernel, shape, [IN_VMEM], [], (value,), flops=0, grant=4 << 20)


def rotate_kernel(sources, choice, split, here_ref, *refs):
    inputs, refs = refs[:sources], refs[sources:]
    w1_ref, but_ref, bu_ref, w5_ref, inv_ref = refs[:5]
    out_ref, *rest = refs[5:]
    tall, first, second = rest[-3:]
    size = but_ref.shape[0] // HALF
    lanes = 2 * size
    fold = inputs[0].shape[0] // TILE
    pairs = size // 2
    half = size * fold

    def gather_rows(q_ref):
        for a in range(pairs):
            for h in range(fold):
                tall[a * TILE : (a + 1) * TILE, h * lanes : (h + 1) * lanes] = q_ref[
                    h * TILE : (h + 1) * TILE, a * lanes : (a + 1) * lanes
                ]

    if sources == 1:
        gather_rows(inputs[0])
    else:
        which = lookup(choice, here_ref[0])
        for i in range(sources):
            pl.when(which == i)(functools.partial(gather_rows, inputs[i]))
    full = w1_ref.shape[0] // 2
    if half == full:
        w1, w5, inverse = w1_ref[...], w5_ref[...], inv_ref[...]
    else:
        wide = fold * lanes
        w1 = jnp.concatenate([w1_ref[:wide, k * full : k * full + half] for k in range(2)], axis=1)
        w5 = jnp.concatenate([w5_ref[k * full : k * full + half, :wide] for k in range(2)], axis=0)
        inverse = inv_ref[:, :half]
    chunk = 8
    parts = TILE // HALF
    for a0 in range(0, pairs, chunk):
        rows = dot(tall[a0 * TILE : (a0 + chunk) * TILE, :], w1)
        for a in range(a0, a0 + chunk):
            for part in range(parts):
                low = (a - a0) * TILE + part * HALF
                for odd in range(2):
                    at = (2 * a + odd) * HALF
                    first[part, at : at + HALF, :] = rows[low : low + HALF, odd * half : (odd + 1) * half]
    but, bu = but_ref[...], bu_ref[...]
    for part in range(parts):
        scaled = (dot(but, first[part].astype(BF16)) * inverse).astype(BF16)
        second[part] = dot(bu, scaled)
    for a in range(pairs):
        for odd in range(2):
            at = (2 * a + odd) * HALF
            value = jnp.concatenate([second[part, at : at + HALF, :] for part in range(parts)], axis=0)
            tall[a * TILE : (a + 1) * TILE, odd * half : (odd + 1) * half] = value.astype(BF16)
    for a0 in range(0, pairs, chunk):
        rows = dot(tall[a0 * TILE : (a0 + chunk) * TILE, :], w5).astype(BF16)
        for a in range(a0, a0 + chunk):
            for h in range(fold):
                value = rows[(a - a0) * TILE : (a - a0 + 1) * TILE, h * lanes : (h + 1) * lanes]
                out_ref[h * TILE : (h + 1) * TILE, a * lanes : (a + 1) * lanes] = value
                low = h * TILE - split
                if split and low >= 0:
                    rest[0][low : low + TILE, a * lanes : (a + 1) * lanes] = value


def rotate(here, choice, inputs, constants, split=0):
    rows, width = inputs[0].shape
    fold = rows // TILE
    size = constants[1].shape[0] // HALF
    shapes = [jax.ShapeDtypeStruct((rows, width), BF16)]
    if split:
        shapes.append(jax.ShapeDtypeStruct((rows - split, width), BF16))
    return call(
        functools.partial(rotate_kernel, len(inputs), choice, split),
        shapes,
        [IN_SMEM] + [IN_VMEM] * (len(inputs) + 5),
        [
            pltpu.VMEM((size // 2 * TILE, 2 * size * fold), BF16),
            pltpu.VMEM((TILE // HALF, size * HALF, size * fold), F32),
            pltpu.VMEM((TILE // HALF, size * HALF, size * fold), F32),
        ],
        (here, *inputs, *constants),
        flops=8 * rows * width * size * fold,
        grant=12 << 20,
    )


def fill(held, units, choices, here_ref):
    at = 0
    for candidates, choice in zip(units, choices):
        rows = candidates[0].shape[0]

        def take(ref, at=at, rows=rows):
            held[at : at + rows, :] = ref[...]

        if len(candidates) == 1:
            take(candidates[0])
        else:
            which = lookup(choice, here_ref[0])
            for i, ref in enumerate(candidates):
                pl.when(which == i)(functools.partial(take, ref))
        at += rows


def products(held, x_ref, kept_ref):
    total = x_ref.shape[0]
    step = min(256, total)
    for t in range(0, total, step):
        kept_ref[:, t : t + step] = lax.dot_general(
            x_ref[t : t + step, :], held[...], (((1,), (1,)), ((), ())), preferred_element_type=F32
        ).T


def grid_lookup(table, z, owner):
    value = lookup([row[0] for row in table], z)
    for o in range(1, len(table[0])):
        value = jnp.where(owner == o, lookup([row[o] for row in table], z), value)
    return value


def aligned(start, rows):
    return pl.ds(pl.multiple_of(start, rows), rows)


def early_kernel(shape, choices, table, piece, here_ref, *refs):
    refs = list(refs)
    units = [[refs.pop(0) for _ in range(n)] for n in shape]
    x_ref, kept_ref, *sent = refs[:-1]
    held = refs[-1]
    fill(held, units, choices, here_ref)
    products(held, x_ref, kept_ref)
    z, x = here_ref[0], here_ref[1]
    layers = len(sent) + 1
    for d, sent_ref in enumerate(sent, 1):
        target = lax.rem(x + d, layers)
        for p in range(len(table) - 1):
            start = grid_lookup(table[p], z, target)
            sent_ref[p * piece : (p + 1) * piece, :] = kept_ref[aligned(start, piece), :].astype(BF16)


def late_kernel(shape, choices, table, piece, here_ref, *refs):
    refs = list(refs)
    units = [[refs.pop(0) for _ in range(n)] for n in shape]
    x_ref, early_ref, kept_ref, *sent = refs[:-1]
    held = refs[-1]
    fill(held, units, choices, here_ref)
    products(held, x_ref, kept_ref)
    z, x = here_ref[0], here_ref[1]
    layers = len(sent) + 1
    for d, sent_ref in enumerate(sent, 1):
        start = grid_lookup(table[-1], z, lax.rem(x + d, layers))
        last = early_ref.shape[0]

        @pl.when(start == last)
        def _(sent_ref=sent_ref):
            sent_ref[...] = kept_ref[...].astype(BF16)

        @pl.when(start != last)
        def _(sent_ref=sent_ref, start=start):
            sent_ref[...] = early_ref[aligned(start, piece), :].astype(BF16)


def finish_kernel(table, places, piece, layers, here_ref, early_ref, late_ref, *refs):
    *received, out_ref = refs
    z, x = here_ref[0], here_ref[1]
    shifts = layers - 1
    first, second = received[:shifts], received[shifts:]
    last = early_ref.shape[0]
    count = len(table)
    for p in range(count):
        start = grid_lookup(table[p], z, x)
        place = aligned(grid_lookup(places[p], z, x), piece)
        if p < count - 1:
            value = early_ref[aligned(start, piece), :]
            for ref in first:
                value = value + ref[p * piece : (p + 1) * piece, :].astype(F32)
            out_ref[place, :] = value
            continue
        other = second[0][...].astype(F32)
        for ref in second[1:]:
            other = other + ref[...].astype(F32)

        @pl.when(start == last)
        def _():
            out_ref[place, :] = late_ref[...] + other

        @pl.when(start != last)
        def _():
            out_ref[place, :] = early_ref[aligned(start, piece), :] + other


def load_kernel(x_ref, out_ref, sem):
    pieces = sem.shape[0]
    step = x_ref.shape[0] // pieces
    copies = []
    for i in range(pieces):
        rows = pl.ds(i * step, step)
        copies.append(pltpu.make_async_copy(x_ref.at[rows], out_ref.at[rows], sem.at[i]))
    for copy in copies:
        copy.start()
    for copy in copies:
        copy.wait()


def resident(x):
    return pl.pallas_call(
        load_kernel,
        out_shape=pltpu.VMEM(x.shape, x.dtype),
        in_specs=[pl.BlockSpec(memory_space=pltpu.HBM)],
        out_specs=IN_VMEM,
        scratch_shapes=[pltpu.SemaphoreType.DMA((8,))],
        compiler_params=pltpu.CompilerParams(vmem_limit_bytes=12 << 20),
        cost_estimate=pl.CostEstimate(
            flops=0, bytes_accessed=2 * x.size * x.dtype.itemsize, transcendentals=0
        ),
    )(x)


def steps(train_grads, queries, bases, eigenvalues):
    blocks, layers, reps = lax.axis_size("blk"), lax.axis_size("layer"), lax.axis_size("rep")
    z, x, rep = lax.axis_index("blk"), lax.axis_index("layer"), lax.axis_index("rep")
    train = train_grads[0]
    own = queries[0, 0]
    base_rows, lanes = bases.shape[1:]
    size = lanes // 2
    rows = own.shape[0]
    fold = rows // TILE
    per_owner = blocks // layers

    plan, arrivals = line_plan(blocks)
    here = jnp.stack([z, x, rep]).astype(jnp.int32)
    splits = 2
    piece = rows // splits

    raw, mixed = {}, {}
    raw[1, 1] = lax.ppermute(own, "blk", plan[1, 1])
    raw[1, 0] = lax.ppermute(own, "blk", plan[1, 0])

    eigen = eigenvalues.reshape(-1, lanes)
    eigen_rows = eigen.shape[0]
    packed = call(
        pack_kernel,
        jax.ShapeDtypeStruct((base_rows + eigen_rows, lanes), F32),
        [IN_VMEM] * 2,
        [],
        (bases[0], eigen),
        flops=0,
        grant=4 << 20,
    )
    pair = [packed]
    for e in range(1, reps):
        pair.append(lax.ppermute(packed, "rep", [(r, (r + e) % reps) for r in range(reps)]))
    pair = jnp.concatenate(pair, axis=0)
    parts = [pair]
    for d in range(1, blocks):
        parts.append(lax.ppermute(pair, "blk", [(a, (a + d) % blocks) for a in range(blocks)]))
    train, here, _ = lax.optimization_barrier((train, here, pair))
    train = resident(train)
    raw[1, 1], train = lax.optimization_barrier((raw[1, 1], train))
    raw[2, 0] = lax.ppermute(raw[1, 1], "blk", plan[2, 0])

    constants = rotation_constants(parts, here, reps, base_rows, eigen_rows, size, fold)
    alone = [0] * blocks
    block_of = [list(range(blocks))] + [[a[j][2] for a in arrivals] for j in range(blocks - 1)]
    source_of = [None] + [[a[j][:2] for a in arrivals] for j in range(blocks - 1)]

    def hop(step, parity, value):
        return lax.ppermute(value, "blk", plan[step, parity])

    mixed[2, 1] = [hop(2, 1, head(raw[1, 0], piece))] if (2, 1) in plan else []
    whole_first, last = rotate(here, alone, [raw[1, 0]], constants, piece)
    if mixed[2, 1]:
        mixed[2, 1].append(hop(2, 1, last))
        if (3, 0) in plan:
            mixed[3, 0] = [hop(3, 0, mixed[2, 1][0])]
    whole_own, = rotate(here, alone, [own], constants)
    units, choices = [[whole_own], [whole_first]], [alone, alone]

    turned_last = {}

    def last_rows(name):
        if name in mixed:
            return mixed[name][1]
        if name not in turned_last:
            turned_last[name] = rotate(here, alone, [raw[name]], constants, piece)[1]
        return turned_last[name]

    def first_rows(name):
        return mixed[name][0] if name in mixed else head(raw[name], piece)

    gate = whole_own
    for j in range(2, blocks):
        names = sorted(set(source_of[j]))
        choice = [names.index(s) for s in source_of[j]]
        if all(n in raw for n in names):
            whole, = rotate(here, choice, [raw[n] for n in names], constants)
            units.append([whole])
            choices.append(choice if len(units[-1]) > 1 else alone)
            gate = whole
            continue
        for step, parity in plan:
            if step > j or (step, parity) in raw:
                continue
            parts = mixed.setdefault((step, parity), [])
            before = (step - 1, 1 - parity)
            while len(parts) < splits:
                value = last_rows(before) if parts else first_rows(before)
                if step > 2:
                    value, _ = lax.optimization_barrier((value, gate))
                parts.append(hop(step, parity, value))
        early_rows, = rotate(here, choice, [first_rows(n) for n in names], constants)
        units += [[early_rows], [last_rows(n) for n in names]]
        choices += [alone, choice]

    count = per_owner * splits
    table = [[[0] * layers for _ in range(blocks)] for _ in range(count)]
    places = [[[0] * layers for _ in range(blocks)] for _ in range(count)]
    for a in range(blocks):
        for o in range(layers):
            mine = [j for j in range(blocks) if block_of[j][a] // per_owner == o]
            for p in range(count):
                j, part = mine[p // splits], p % splits
                table[p][a][o] = j * rows + part * piece
                places[p][a][o] = block_of[j][a] % per_owner * rows + part * piece

    def shifted(sent):
        return [
            lax.ppermute(s, "layer", [(o, (o + d) % layers) for o in range(layers)])
            for d, s in enumerate(sent, 1)
        ]

    def scores(kernel, units, choices, inputs, sent_rows, grant):
        held = sum(u[0].shape[0] for u in units)
        total, width = train.shape
        flat = [w for u in units for w in u] + [train] + inputs
        sent_shape = jax.ShapeDtypeStruct((sent_rows, total), BF16)
        return call(
            functools.partial(kernel, [len(u) for u in units], choices, table, piece),
            [jax.ShapeDtypeStruct((held, total), F32)] + [sent_shape] * (layers - 1),
            [IN_SMEM] + [IN_VMEM] * len(flat),
            [pltpu.VMEM((held, width), BF16)],
            (here, *flat),
            flops=2 * held * total * width,
            grant=grant,
        )

    early, *sent = scores(early_kernel, units[:-1], choices[:-1], [], (count - 1) * piece, 16 << 20)
    first = shifted(sent)
    late, *sent = scores(late_kernel, units[-1:], choices[-1:], [early], piece, 12 << 20)
    second = shifted(sent)
    out = call(
        functools.partial(finish_kernel, table, places, piece, layers),
        jax.ShapeDtypeStruct((per_owner * rows, train.shape[0]), F32),
        [IN_SMEM] + [IN_VMEM] * (2 + 2 * (layers - 1)),
        [],
        (here, early, late, *first, *second),
        flops=per_owner * rows * train.shape[0],
        grant=12 << 20,
    )
    return out[None]


def solution(mesh):
    return jax.shard_map(
        steps,
        mesh=mesh,
        in_specs=(
            P("layer", ("groups", "blk"), None),
            P("layer", "rep", ("groups", "blk"), None),
            P("layer", ("blk", "rep"), None),
            P("layer", ("blk", "rep")),
        ),
        out_specs=P("rep", "layer", ("groups", "blk")),
        check_vma=False,
    )
```

```python
import functools

import jax
import jax.numpy as jnp
from jax import lax
from jax.experimental import pallas as pl
from jax.experimental.pallas import tpu as pltpu
from jax.sharding import PartitionSpec as P

TILE = 16
HALF = 8
BF16, F32 = jnp.bfloat16, jnp.float32
IN_VMEM = pl.BlockSpec(memory_space=pltpu.VMEM)
IN_SMEM = pl.BlockSpec(memory_space=pltpu.SMEM)


def dot(a, b):
    return jnp.dot(a, b, preferred_element_type=F32)


def call(kernel, out_shape, in_specs, scratch, args, flops, grant):
    outs = out_shape if isinstance(out_shape, (list, tuple)) else [out_shape]
    moved = sum(a.size * a.dtype.itemsize for a in list(args) + list(outs))
    return pl.pallas_call(
        kernel,
        out_shape=out_shape,
        in_specs=in_specs,
        out_specs=jax.tree.map(lambda _: IN_VMEM, out_shape),
        scratch_shapes=scratch,
        compiler_params=pltpu.CompilerParams(vmem_limit_bytes=grant),
        cost_estimate=pl.CostEstimate(flops=flops, bytes_accessed=moved, transcendentals=0),
    )(*args)


def line_plan(count):
    plan, arrivals = {}, [[] for _ in range(count)]
    for step in range(1, count):
        for parity in range(2):
            pairs = []
            for low in range(parity, count - 1, 2):
                high = low + 1
                if low - (step - 1) >= 0:
                    pairs.append((low, high))
                    arrivals[high].append((step, parity, low - (step - 1)))
                if high + (step - 1) < count:
                    pairs.append((high, low))
                    arrivals[low].append((step, parity, high + (step - 1)))
            if pairs:
                plan[step, parity] = pairs
    return plan, arrivals


def lookup(values, index):
    value = jnp.int32(values[0])
    for i, v in enumerate(values[1:], 1):
        if v != values[0]:
            value = jnp.where(index == i, jnp.int32(v), value)
    return value


def spread(matrix, rows, cols, keep):
    size = matrix.shape[0]
    r = lax.broadcasted_iota(jnp.int32, (rows, size), 0)
    i = lax.broadcasted_iota(jnp.int32, (rows, size), 1)
    j = lax.broadcasted_iota(jnp.int32, (size, cols), 0)
    c = lax.broadcasted_iota(jnp.int32, (size, cols), 1)
    down = jnp.where(lax.rem(r, size) == i, 1.0, 0.0).astype(BF16)
    along = jnp.where(lax.rem(c, size) == j, 1.0, 0.0).astype(BF16)
    full = dot(dot(down, matrix.astype(BF16)).astype(BF16), along)
    block_row = lax.broadcasted_iota(jnp.int32, (rows, cols), 0) // size
    block_col = lax.broadcasted_iota(jnp.int32, (rows, cols), 1) // size
    return jnp.where(keep(block_row, block_col), full, 0.0).astype(BF16)


def comb(matrix, out_ref):
    size = matrix.shape[0]
    wide = size * HALF
    j = lax.broadcasted_iota(jnp.int32, (size, wide), 0)
    c = lax.broadcasted_iota(jnp.int32, (size, wide), 1)
    rows = dot(matrix.astype(BF16), jnp.where(c // HALF == j, 1.0, 0.0).astype(BF16))
    r = lax.broadcasted_iota(jnp.int32, (HALF, wide), 0)
    c = lax.broadcasted_iota(jnp.int32, (HALF, wide), 1)
    keep = r == lax.rem(c, HALF)
    for i in range(0, size, 2):
        pair = [
            jnp.where(keep, jnp.broadcast_to(rows[k : k + 1], (HALF, wide)), 0.0) for k in (i, i + 1)
        ]
        out_ref[i * HALF : (i + 2) * HALF, :] = jnp.concatenate(pair, axis=0).astype(BF16)


def prep_kernel(shape, here_ref, *refs):
    count, reps, base_rows, eigen_rows, fold = shape
    parts = refs[:count]
    w1_ref, but_ref, bu_ref, w5_ref, inv_ref, base3, eigen3, base, eigen, pad = refs[count:]
    z, rep = here_ref[0], here_ref[2]
    each = base_rows + eigen_rows
    for d in range(count):
        for e in range(reps):
            source = lax.rem(z + count - d, count) * reps + lax.rem(rep + reps - e, reps)
            base3[source] = parts[d][e * each : e * each + base_rows, :]
            eigen3[source] = parts[d][e * each + base_rows : (e + 1) * each, :]
    for s in range(count * reps):
        base[s * base_rows : (s + 1) * base_rows, :] = base3[s]
        eigen[s * eigen_rows : (s + 1) * eigen_rows, :] = eigen3[s]
    size = base.shape[0]
    basis = base[...]
    left, right = basis[:, :size], basis[:, size:]
    turned = basis.T
    left_t, right_t = turned[:size], turned[size:]
    wide = 2 * size * fold
    w1_ref[...] = spread(
        right, wide, wide, lambda r, c: (r // 2 == lax.rem(c, fold)) & (lax.rem(r, 2) == c // fold)
    )
    w5_ref[...] = spread(
        right_t, wide, wide, lambda r, c: (c // 2 == lax.rem(r, fold)) & (lax.rem(c, 2) == r // fold)
    )
    comb(left_t, but_ref)
    comb(left, bu_ref)
    values = eigen[...]
    inverse = 1.0 / (values + 0.1 * (jnp.sum(values) / (size * size)))
    shifted = pltpu.roll(inverse, size, 1)
    lane = lax.broadcasted_iota(jnp.int32, inverse.shape, 1)
    pad[pl.ds(0, size // 2, stride=2), :] = jnp.where(lane < size, inverse, shifted)
    pad[pl.ds(1, size // 2, stride=2), :] = jnp.where(lane < size, shifted, inverse)
    for i in range(size):
        row = jnp.broadcast_to(pad[i : i + 1, :], (HALF, 2 * size))
        for h in range(fold // 2):
            inv_ref[i * HALF : (i + 1) * HALF, h * 2 * size : (h + 1) * 2 * size] = row


def rotation_constants(parts, here, reps, base_rows, eigen_rows, size, fold):
    count = len(parts)
    wide, tall = 2 * size * fold, HALF * size
    shard = count * reps
    return call(
        functools.partial(prep_kernel, (count, reps, base_rows, eigen_rows, fold)),
        [
            jax.ShapeDtypeStruct((wide, wide), BF16),
            jax.ShapeDtypeStruct((tall, tall), BF16),
            jax.ShapeDtypeStruct((tall, tall), BF16),
            jax.ShapeDtypeStruct((wide, wide), BF16),
            jax.ShapeDtypeStruct((tall, size * fold), F32),
        ],
        [IN_SMEM] + [IN_VMEM] * count,
        [
            pltpu.VMEM((shard, base_rows, 2 * size), F32),
            pltpu.VMEM((shard, eigen_rows, 2 * size), F32),
            pltpu.VMEM((size, 2 * size), F32),
            pltpu.VMEM((size // 2, 2 * size), F32),
            pltpu.VMEM((size, 2 * size), F32),
        ],
        (here, *parts),
        flops=2 * wide * wide * 2 * size,
        grant=12 << 20,
    )


def pack_kernel(bases_ref, eigen_ref, out_ref):
    rows = bases_ref.shape[0]
    out_ref[:rows, :] = bases_ref[...].astype(F32)
    out_ref[rows:, :] = eigen_ref[...]


def head_kernel(rows_ref, out_ref):
    out_ref[...] = rows_ref[: out_ref.shape[0], :]


def head(value, rows):
    shape = jax.ShapeDtypeStruct((rows, value.shape[1]), value.dtype)
    return call(head_kernel, shape, [IN_VMEM], [], (value,), flops=0, grant=4 << 20)


def turn(inputs, choice, here_ref, constants, scratch, write):
    w1_ref, but_ref, bu_ref, w5_ref, inv_ref = constants
    tall, first, second = scratch
    size = but_ref.shape[0] // HALF
    lanes = 2 * size
    fold = inputs[0].shape[0] // TILE
    pairs = size // 2
    half = size * fold

    def gather_rows(q_ref):
        for a in range(pairs):
            for h in range(fold):
                tall[a * TILE : (a + 1) * TILE, h * lanes : (h + 1) * lanes] = q_ref[
                    h * TILE : (h + 1) * TILE, a * lanes : (a + 1) * lanes
                ]

    if len(inputs) == 1:
        gather_rows(inputs[0])
    else:
        which = lookup(choice, here_ref[0])
        for i in range(len(inputs)):
            pl.when(which == i)(functools.partial(gather_rows, inputs[i]))
    full = w1_ref.shape[0] // 2
    if half == full:
        w1, w5, inverse = w1_ref[...], w5_ref[...], inv_ref[...]
    else:
        wide = fold * lanes
        w1 = jnp.concatenate([w1_ref[:wide, k * full : k * full + half] for k in range(2)], axis=1)
        w5 = jnp.concatenate([w5_ref[k * full : k * full + half, :wide] for k in range(2)], axis=0)
        inverse = inv_ref[:, :half]
    chunk = 8
    parts = TILE // HALF
    for a0 in range(0, pairs, chunk):
        rows = dot(tall[a0 * TILE : (a0 + chunk) * TILE, :], w1)
        for a in range(a0, a0 + chunk):
            for part in range(parts):
                low = (a - a0) * TILE + part * HALF
                for odd in range(2):
                    at = (2 * a + odd) * HALF
                    first[part, at : at + HALF, :] = rows[low : low + HALF, odd * half : (odd + 1) * half]
    but, bu = but_ref[...], bu_ref[...]
    for part in range(parts):
        scaled = (dot(but, first[part].astype(BF16)) * inverse).astype(BF16)
        second[part] = dot(bu, scaled)
    for a in range(pairs):
        for odd in range(2):
            at = (2 * a + odd) * HALF
            value = jnp.concatenate([second[part, at : at + HALF, :] for part in range(parts)], axis=0)
            tall[a * TILE : (a + 1) * TILE, odd * half : (odd + 1) * half] = value.astype(BF16)
    for a0 in range(0, pairs, chunk):
        rows = dot(tall[a0 * TILE : (a0 + chunk) * TILE, :], w5).astype(BF16)
        for a in range(a0, a0 + chunk):
            for h in range(fold):
                value = rows[(a - a0) * TILE : (a - a0 + 1) * TILE, h * lanes : (h + 1) * lanes]
                write(h * TILE, a * lanes, value)


def rotate_kernel(sources, choice, split, here_ref, *refs):
    inputs, refs = refs[:sources], refs[sources:]
    out_ref, *rest = refs[5:]

    def write(row, lane, value):
        rows, lanes = value.shape
        out_ref[row : row + rows, lane : lane + lanes] = value
        if split and row >= split:
            rest[0][row - split : row - split + rows, lane : lane + lanes] = value

    turn(inputs, choice, here_ref, refs[:5], rest[-3:], write)


def turn_scratch(rows, constants):
    size = constants[1].shape[0] // HALF
    fold = rows // TILE
    return [
        pltpu.VMEM((size // 2 * TILE, 2 * size * fold), BF16),
        pltpu.VMEM((TILE // HALF, size * HALF, size * fold), F32),
        pltpu.VMEM((TILE // HALF, size * HALF, size * fold), F32),
    ]


def rotate(here, choice, inputs, constants, split=0):
    rows, width = inputs[0].shape
    fold = rows // TILE
    size = constants[1].shape[0] // HALF
    shapes = [jax.ShapeDtypeStruct((rows, width), BF16)]
    if split:
        shapes.append(jax.ShapeDtypeStruct((rows - split, width), BF16))
    return call(
        functools.partial(rotate_kernel, len(inputs), choice, split),
        shapes,
        [IN_SMEM] + [IN_VMEM] * (len(inputs) + 5),
        turn_scratch(rows, constants),
        (here, *inputs, *constants),
        flops=8 * rows * width * size * fold,
        grant=12 << 20,
    )


def fill(held, units, choices, here_ref):
    at = 0
    for candidates, choice in zip(units, choices):
        rows = candidates[0].shape[0]

        def take(ref, at=at, rows=rows):
            held[at : at + rows, :] = ref[...]

        if len(candidates) == 1:
            take(candidates[0])
        else:
            which = lookup(choice, here_ref[0])
            for i, ref in enumerate(candidates):
                pl.when(which == i)(functools.partial(take, ref))
        at += rows


def products(held, x_ref, kept_ref):
    total = x_ref.shape[0]
    step = min(256, total)
    for t in range(0, total, step):
        kept_ref[:, t : t + step] = lax.dot_general(
            x_ref[t : t + step, :], held[...], (((1,), (1,)), ((), ())), preferred_element_type=F32
        ).T


def grid_lookup(table, z, owner):
    value = lookup([row[0] for row in table], z)
    for o in range(1, len(table[0])):
        value = jnp.where(owner == o, lookup([row[o] for row in table], z), value)
    return value


def aligned(start, rows):
    return pl.ds(pl.multiple_of(start, rows), rows)


def early_kernel(shape, choices, table, piece, raw_choice, here_ref, *refs):
    refs = list(refs)
    units = [[refs.pop(0) for _ in range(n)] for n in shape]
    x_ref = refs.pop(0)
    inputs = [refs.pop(0) for _ in range(len(set(raw_choice)))]
    constants = [refs.pop(0) for _ in range(5)]
    *scratch, held = refs[-4:]
    kept_ref, *sent = refs[:-4]
    fill(held, units, choices, here_ref)
    base = held.shape[0] - piece

    def write(row, lane, value):
        rows, lanes = value.shape
        held[base + row : base + row + rows, lane : lane + lanes] = value

    turn(inputs, raw_choice, here_ref, constants, scratch, write)
    products(held, x_ref, kept_ref)
    z, x = here_ref[0], here_ref[1]
    layers = len(sent) + 1
    for d, sent_ref in enumerate(sent, 1):
        target = lax.rem(x + d, layers)
        for p in range(len(table) - 1):
            start = grid_lookup(table[p], z, target)
            sent_ref[p * piece : (p + 1) * piece, :] = kept_ref[aligned(start, piece), :].astype(BF16)


def late_kernel(shape, choices, table, piece, here_ref, *refs):
    refs = list(refs)
    units = [[refs.pop(0) for _ in range(n)] for n in shape]
    x_ref, early_ref, kept_ref, *sent = refs[:-1]
    held = refs[-1]
    fill(held, units, choices, here_ref)
    products(held, x_ref, kept_ref)
    z, x = here_ref[0], here_ref[1]
    layers = len(sent) + 1
    for d, sent_ref in enumerate(sent, 1):
        start = grid_lookup(table[-1], z, lax.rem(x + d, layers))
        last = early_ref.shape[0]

        @pl.when(start == last)
        def _(sent_ref=sent_ref):
            sent_ref[...] = kept_ref[...].astype(BF16)

        @pl.when(start != last)
        def _(sent_ref=sent_ref, start=start):
            sent_ref[...] = early_ref[aligned(start, piece), :].astype(BF16)


def first_finish_kernel(table, places, piece, here_ref, early_ref, *refs):
    *received, out_ref = refs
    z, x = here_ref[0], here_ref[1]
    for p in range(len(table) - 1):
        value = early_ref[aligned(grid_lookup(table[p], z, x), piece), :]
        for ref in received:
            value = value + ref[p * piece : (p + 1) * piece, :].astype(F32)
        out_ref[aligned(grid_lookup(places[p], z, x), piece), :] = value


def last_finish_kernel(table, places, piece, here_ref, _, early_ref, late_ref, *refs):
    *received, out_ref, total, sem = refs
    z, x = here_ref[0], here_ref[1]
    start = grid_lookup(table[-1], z, x)
    last = early_ref.shape[0]
    other = received[0][...].astype(F32)
    for ref in received[1:]:
        other = other + ref[...].astype(F32)

    @pl.when(start == last)
    def _():
        total[...] = late_ref[...] + other

    @pl.when(start != last)
    def _():
        total[...] = early_ref[aligned(start, piece), :] + other

    place = aligned(grid_lookup(places[-1], z, x), piece)
    copy = pltpu.make_async_copy(total, out_ref.at[place], sem)
    copy.start()
    copy.wait()


def load_kernel(x_ref, out_ref, sem):
    pieces = sem.shape[0]
    step = x_ref.shape[0] // pieces
    copies = []
    for i in range(pieces):
        rows = pl.ds(i * step, step)
        copies.append(pltpu.make_async_copy(x_ref.at[rows], out_ref.at[rows], sem.at[i]))
    for copy in copies:
        copy.start()
    for copy in copies:
        copy.wait()


def resident(x):
    return pl.pallas_call(
        load_kernel,
        out_shape=pltpu.VMEM(x.shape, x.dtype),
        in_specs=[pl.BlockSpec(memory_space=pltpu.HBM)],
        out_specs=IN_VMEM,
        scratch_shapes=[pltpu.SemaphoreType.DMA((8,))],
        compiler_params=pltpu.CompilerParams(vmem_limit_bytes=12 << 20),
        cost_estimate=pl.CostEstimate(
            flops=0, bytes_accessed=2 * x.size * x.dtype.itemsize, transcendentals=0
        ),
    )(x)


def steps(train_grads, queries, bases, eigenvalues):
    blocks, layers, reps = lax.axis_size("blk"), lax.axis_size("layer"), lax.axis_size("rep")
    z, x, rep = lax.axis_index("blk"), lax.axis_index("layer"), lax.axis_index("rep")
    train = train_grads[0]
    own = queries[0, 0]
    base_rows, lanes = bases.shape[1:]
    size = lanes // 2
    rows = own.shape[0]
    fold = rows // TILE
    per_owner = blocks // layers

    plan, arrivals = line_plan(blocks)
    here = jnp.stack([z, x, rep]).astype(jnp.int32)
    splits = 2
    piece = rows // splits

    raw, mixed = {}, {}
    raw[1, 1] = lax.ppermute(own, "blk", plan[1, 1])
    raw[1, 0] = lax.ppermute(own, "blk", plan[1, 0])

    eigen = eigenvalues.reshape(-1, lanes)
    eigen_rows = eigen.shape[0]
    packed = call(
        pack_kernel,
        jax.ShapeDtypeStruct((base_rows + eigen_rows, lanes), F32),
        [IN_VMEM] * 2,
        [],
        (bases[0], eigen),
        flops=0,
        grant=4 << 20,
    )
    pair = [packed]
    for e in range(1, reps):
        pair.append(lax.ppermute(packed, "rep", [(r, (r + e) % reps) for r in range(reps)]))
    pair = jnp.concatenate(pair, axis=0)
    parts = [pair]
    for d in range(1, blocks):
        parts.append(lax.ppermute(pair, "blk", [(a, (a + d) % blocks) for a in range(blocks)]))
    train, here, _ = lax.optimization_barrier((train, here, pair))
    train = resident(train)
    raw[1, 1], train = lax.optimization_barrier((raw[1, 1], train))
    raw[2, 0] = lax.ppermute(raw[1, 1], "blk", plan[2, 0])

    constants = rotation_constants(parts, here, reps, base_rows, eigen_rows, size, fold)
    alone = [0] * blocks
    block_of = [list(range(blocks))] + [[a[j][2] for a in arrivals] for j in range(blocks - 1)]
    source_of = [None] + [[a[j][:2] for a in arrivals] for j in range(blocks - 1)]

    def hop(step, parity, value):
        return lax.ppermute(value, "blk", plan[step, parity])

    mixed[2, 1] = [hop(2, 1, head(raw[1, 0], piece))] if (2, 1) in plan else []
    whole_first, last = rotate(here, alone, [raw[1, 0]], constants, piece)
    if mixed[2, 1]:
        mixed[2, 1].append(hop(2, 1, last))
        if (3, 0) in plan:
            mixed[3, 0] = [hop(3, 0, mixed[2, 1][0])]
    whole_own, = rotate(here, alone, [own], constants)
    units, choices = [[whole_own], [whole_first]], [alone, alone]

    turned_last = {}

    def last_rows(name):
        if name in mixed:
            return mixed[name][1]
        if name not in turned_last:
            turned_last[name] = rotate(here, alone, [raw[name]], constants, piece)[1]
        return turned_last[name]

    def first_rows(name):
        return mixed[name][0] if name in mixed else head(raw[name], piece)

    gate = whole_own
    late_raw = []
    for j in range(2, blocks):
        names = sorted(set(source_of[j]))
        choice = [names.index(s) for s in source_of[j]]
        if all(n in raw for n in names):
            whole, = rotate(here, choice, [raw[n] for n in names], constants)
            units.append([whole])
            choices.append(choice if len(units[-1]) > 1 else alone)
            gate = whole
            continue
        for step, parity in plan:
            if step > j or (step, parity) in raw:
                continue
            parts = mixed.setdefault((step, parity), [])
            before = (step - 1, 1 - parity)
            while len(parts) < splits:
                value = last_rows(before) if parts else first_rows(before)
                if step > 2:
                    value, _ = lax.optimization_barrier((value, gate))
                parts.append(hop(step, parity, value))
        late_raw.append((j, choice, [first_rows(n) for n in names]))
        units += [None, [last_rows(n) for n in names]]
        choices += [alone, choice]
    for j, choice, values in late_raw[:-1]:
        turned_piece, = rotate(here, choice, values, constants)
        units[units.index(None)] = [turned_piece]
    raw_choice, raw_values = late_raw[-1][1:]
    units.remove(None)
    choices.pop(-2)

    count = per_owner * splits
    table = [[[0] * layers for _ in range(blocks)] for _ in range(count)]
    places = [[[0] * layers for _ in range(blocks)] for _ in range(count)]
    for a in range(blocks):
        for o in range(layers):
            mine = [j for j in range(blocks) if block_of[j][a] // per_owner == o]
            for p in range(count):
                j, part = mine[p // splits], p % splits
                table[p][a][o] = j * rows + part * piece
                places[p][a][o] = block_of[j][a] % per_owner * rows + part * piece

    def shifted(sent):
        return [
            lax.ppermute(s, "layer", [(o, (o + d) % layers) for o in range(layers)])
            for d, s in enumerate(sent, 1)
        ]

    total, width = train.shape

    def scores(kernel, units, choices, extra, held, sent_rows, scratch, grant):
        flat = [w for u in units for w in u] + [train] + extra
        sent_shape = jax.ShapeDtypeStruct((sent_rows, total), BF16)
        return call(
            functools.partial(kernel, [len(u) for u in units], choices, table, piece),
            [jax.ShapeDtypeStruct((held, total), F32)] + [sent_shape] * (layers - 1),
            [IN_SMEM] + [IN_VMEM] * len(flat),
            scratch + [pltpu.VMEM((held, width), BF16)],
            (here, *flat),
            flops=2 * held * total * width,
            grant=grant,
        )

    early, *sent = scores(
        lambda shape, choices, table, piece, *refs: early_kernel(
            shape, choices, table, piece, raw_choice, *refs
        ),
        units[:-1],
        choices[:-1],
        [*raw_values, *constants],
        blocks * rows - piece,
        (count - 1) * piece,
        turn_scratch(piece, constants),
        16 << 20,
    )
    first = shifted(sent)
    late, *sent = scores(
        late_kernel, units[-1:], choices[-1:], [early], piece, piece, [], 12 << 20
    )
    second = shifted(sent)
    out_shape = jax.ShapeDtypeStruct((per_owner * rows, total), F32)
    out = call(
        functools.partial(first_finish_kernel, table, places, piece),
        out_shape,
        [IN_SMEM] + [IN_VMEM] * layers,
        [],
        (here, early, *first),
        flops=per_owner * rows * total,
        grant=8 << 20,
    )
    in_hbm = pl.BlockSpec(memory_space=pltpu.HBM)
    out = pl.pallas_call(
        functools.partial(last_finish_kernel, table, places, piece),
        out_shape=out_shape,
        in_specs=[IN_SMEM, in_hbm] + [IN_VMEM] * (1 + layers),
        out_specs=in_hbm,
        scratch_shapes=[pltpu.VMEM((piece, total), F32), pltpu.SemaphoreType.DMA],
        input_output_aliases={1: 0},
        compiler_params=pltpu.CompilerParams(vmem_limit_bytes=8 << 20),
    )(here, out, early, late, *second)
    return out[None]


def solution(mesh):
    return jax.shard_map(
        steps,
        mesh=mesh,
        in_specs=(
            P("layer", ("groups", "blk"), None),
            P("layer", "rep", ("groups", "blk"), None),
            P("layer", ("blk", "rep"), None),
            P("layer", ("blk", "rep")),
        ),
        out_specs=P("rep", "layer", ("groups", "blk")),
        check_vma=False,
    )
```

```python
import functools

import jax
import jax.numpy as jnp
from jax import lax
from jax.experimental import pallas as pl
from jax.experimental.pallas import tpu as pltpu
from jax.sharding import PartitionSpec as P

TILE = 16
HALF = 8
BF16, F32 = jnp.bfloat16, jnp.float32
IN_VMEM = pl.BlockSpec(memory_space=pltpu.VMEM)


class Place:
    def __getitem__(self, axis):
        return lax.axis_index(("blk", "layer", "rep")[axis])


PLACE = Place()


def dot(a, b):
    return jnp.dot(a, b, preferred_element_type=F32)


def call(kernel, out_shape, in_specs, scratch, args, flops, grant):
    outs = out_shape if isinstance(out_shape, (list, tuple)) else [out_shape]
    moved = sum(a.size * a.dtype.itemsize for a in list(args) + list(outs))
    return pl.pallas_call(
        kernel,
        out_shape=out_shape,
        in_specs=in_specs,
        out_specs=jax.tree.map(lambda _: IN_VMEM, out_shape),
        scratch_shapes=scratch,
        compiler_params=pltpu.CompilerParams(vmem_limit_bytes=grant),
        cost_estimate=pl.CostEstimate(flops=flops, bytes_accessed=moved, transcendentals=0),
    )(*args)


def line_plan(count):
    plan, arrivals = {}, [[] for _ in range(count)]
    for step in range(1, count):
        for parity in range(2):
            pairs = []
            for low in range(parity, count - 1, 2):
                high = low + 1
                if low - (step - 1) >= 0:
                    pairs.append((low, high))
                    arrivals[high].append((step, parity, low - (step - 1)))
                if high + (step - 1) < count:
                    pairs.append((high, low))
                    arrivals[low].append((step, parity, high + (step - 1)))
            if pairs:
                plan[step, parity] = pairs
    return plan, arrivals


def lookup(values, index):
    value = jnp.int32(values[0])
    for i, v in enumerate(values[1:], 1):
        if v != values[0]:
            value = jnp.where(index == i, jnp.int32(v), value)
    return value


def spread(matrix, rows, cols, keep):
    size = matrix.shape[0]
    r = lax.broadcasted_iota(jnp.int32, (rows, size), 0)
    i = lax.broadcasted_iota(jnp.int32, (rows, size), 1)
    j = lax.broadcasted_iota(jnp.int32, (size, cols), 0)
    c = lax.broadcasted_iota(jnp.int32, (size, cols), 1)
    down = jnp.where(lax.rem(r, size) == i, 1.0, 0.0).astype(BF16)
    along = jnp.where(lax.rem(c, size) == j, 1.0, 0.0).astype(BF16)
    full = dot(dot(down, matrix.astype(BF16)).astype(BF16), along)
    block_row = lax.broadcasted_iota(jnp.int32, (rows, cols), 0) // size
    block_col = lax.broadcasted_iota(jnp.int32, (rows, cols), 1) // size
    return jnp.where(keep(block_row, block_col), full, 0.0).astype(BF16)


def comb(matrix, out_ref):
    size = matrix.shape[0]
    wide = size * HALF
    j = lax.broadcasted_iota(jnp.int32, (size, wide), 0)
    c = lax.broadcasted_iota(jnp.int32, (size, wide), 1)
    rows = dot(matrix.astype(BF16), jnp.where(c // HALF == j, 1.0, 0.0).astype(BF16))
    r = lax.broadcasted_iota(jnp.int32, (HALF, wide), 0)
    c = lax.broadcasted_iota(jnp.int32, (HALF, wide), 1)
    keep = r == lax.rem(c, HALF)
    for i in range(0, size, 2):
        pair = [
            jnp.where(keep, jnp.broadcast_to(rows[k : k + 1], (HALF, wide)), 0.0) for k in (i, i + 1)
        ]
        out_ref[i * HALF : (i + 2) * HALF, :] = jnp.concatenate(pair, axis=0).astype(BF16)


def prep_kernel(shape, here_ref, *refs):
    count, reps, base_rows, eigen_rows, fold = shape
    parts = refs[:count]
    w1_ref, but_ref, bu_ref, w5_ref, inv_ref, base3, eigen3, base, eigen, pad = refs[count:]
    z, rep = here_ref[0], here_ref[2]
    each = base_rows + eigen_rows
    for d in range(count):
        for e in range(reps):
            source = lax.rem(z + count - d, count) * reps + lax.rem(rep + reps - e, reps)
            base3[source] = parts[d][e * each : e * each + base_rows, :]
            eigen3[source] = parts[d][e * each + base_rows : (e + 1) * each, :]
    for s in range(count * reps):
        base[s * base_rows : (s + 1) * base_rows, :] = base3[s]
        eigen[s * eigen_rows : (s + 1) * eigen_rows, :] = eigen3[s]
    size = base.shape[0]
    basis = base[...]
    left, right = basis[:, :size], basis[:, size:]
    turned = basis.T
    left_t, right_t = turned[:size], turned[size:]
    wide = 2 * size * fold
    w1_ref[...] = spread(
        right, wide, wide, lambda r, c: (r // 2 == lax.rem(c, fold)) & (lax.rem(r, 2) == c // fold)
    )
    w5_ref[...] = spread(
        right_t, wide, wide, lambda r, c: (c // 2 == lax.rem(r, fold)) & (lax.rem(c, 2) == r // fold)
    )
    comb(left_t, but_ref)
    comb(left, bu_ref)
    values = eigen[...]
    inverse = 1.0 / (values + 0.1 * (jnp.sum(values) / (size * size)))
    shifted = pltpu.roll(inverse, size, 1)
    lane = lax.broadcasted_iota(jnp.int32, inverse.shape, 1)
    pad[pl.ds(0, size // 2, stride=2), :] = jnp.where(lane < size, inverse, shifted)
    pad[pl.ds(1, size // 2, stride=2), :] = jnp.where(lane < size, shifted, inverse)
    for i in range(size):
        row = jnp.broadcast_to(pad[i : i + 1, :], (HALF, 2 * size))
        for h in range(fold // 2):
            inv_ref[i * HALF : (i + 1) * HALF, h * 2 * size : (h + 1) * 2 * size] = row


def rotation_constants(parts, reps, base_rows, eigen_rows, size, fold):
    count = len(parts)
    wide, tall = 2 * size * fold, HALF * size
    shard = count * reps
    return call(
        functools.partial(prep_kernel, (count, reps, base_rows, eigen_rows, fold), PLACE),
        [
            jax.ShapeDtypeStruct((wide, wide), BF16),
            jax.ShapeDtypeStruct((tall, tall), BF16),
            jax.ShapeDtypeStruct((tall, tall), BF16),
            jax.ShapeDtypeStruct((wide, wide), BF16),
            jax.ShapeDtypeStruct((tall, size * fold), F32),
        ],
        [IN_VMEM] * count,
        [
            pltpu.VMEM((shard, base_rows, 2 * size), F32),
            pltpu.VMEM((shard, eigen_rows, 2 * size), F32),
            pltpu.VMEM((size, 2 * size), F32),
            pltpu.VMEM((size // 2, 2 * size), F32),
            pltpu.VMEM((size, 2 * size), F32),
        ],
        tuple(parts),
        flops=2 * wide * wide * 2 * size,
        grant=12 << 20,
    )


def pack_kernel(bases_ref, eigen_ref, out_ref):
    rows = bases_ref.shape[0]
    out_ref[:rows, :] = bases_ref[...].astype(F32)
    out_ref[rows:, :] = eigen_ref[...]


def head_kernel(rows_ref, out_ref):
    out_ref[...] = rows_ref[: out_ref.shape[0], :]


def head(value, rows):
    shape = jax.ShapeDtypeStruct((rows, value.shape[1]), value.dtype)
    return call(head_kernel, shape, [IN_VMEM], [], (value,), flops=0, grant=4 << 20)


def turn(inputs, choice, here_ref, constants, scratch, write):
    w1_ref, but_ref, bu_ref, w5_ref, inv_ref = constants
    tall, first, second = scratch
    size = but_ref.shape[0] // HALF
    lanes = 2 * size
    fold = inputs[0].shape[0] // TILE
    pairs = size // 2
    half = size * fold

    def gather_rows(q_ref):
        for a in range(pairs):
            for h in range(fold):
                tall[a * TILE : (a + 1) * TILE, h * lanes : (h + 1) * lanes] = q_ref[
                    h * TILE : (h + 1) * TILE, a * lanes : (a + 1) * lanes
                ]

    if len(inputs) == 1:
        gather_rows(inputs[0])
    else:
        which = lookup(choice, here_ref[0])
        for i in range(len(inputs)):
            pl.when(which == i)(functools.partial(gather_rows, inputs[i]))
    full = w1_ref.shape[0] // 2
    if half == full:
        w1, w5, inverse = w1_ref[...], w5_ref[...], inv_ref[...]
    else:
        wide = fold * lanes
        w1 = jnp.concatenate([w1_ref[:wide, k * full : k * full + half] for k in range(2)], axis=1)
        w5 = jnp.concatenate([w5_ref[k * full : k * full + half, :wide] for k in range(2)], axis=0)
        inverse = inv_ref[:, :half]
    chunk = 8
    parts = TILE // HALF
    for a0 in range(0, pairs, chunk):
        rows = dot(tall[a0 * TILE : (a0 + chunk) * TILE, :], w1)
        for a in range(a0, a0 + chunk):
            for part in range(parts):
                low = (a - a0) * TILE + part * HALF
                for odd in range(2):
                    at = (2 * a + odd) * HALF
                    first[part, at : at + HALF, :] = rows[low : low + HALF, odd * half : (odd + 1) * half]
    but, bu = but_ref[...], bu_ref[...]
    for part in range(parts):
        scaled = (dot(but, first[part].astype(BF16)) * inverse).astype(BF16)
        second[part] = dot(bu, scaled)
    for a in range(pairs):
        for odd in range(2):
            at = (2 * a + odd) * HALF
            value = jnp.concatenate([second[part, at : at + HALF, :] for part in range(parts)], axis=0)
            tall[a * TILE : (a + 1) * TILE, odd * half : (odd + 1) * half] = value.astype(BF16)
    for a0 in range(0, pairs, chunk):
        rows = dot(tall[a0 * TILE : (a0 + chunk) * TILE, :], w5).astype(BF16)
        for a in range(a0, a0 + chunk):
            for h in range(fold):
                value = rows[(a - a0) * TILE : (a - a0 + 1) * TILE, h * lanes : (h + 1) * lanes]
                write(h * TILE, a * lanes, value)


def rotate_kernel(sources, choice, split, here_ref, *refs):
    inputs, refs = refs[:sources], refs[sources:]
    out_ref, *rest = refs[5:]

    def write(row, lane, value):
        rows, lanes = value.shape
        out_ref[row : row + rows, lane : lane + lanes] = value
        if split and row >= split:
            rest[0][row - split : row - split + rows, lane : lane + lanes] = value

    turn(inputs, choice, here_ref, refs[:5], rest[-3:], write)


def turn_scratch(rows, constants):
    size = constants[1].shape[0] // HALF
    fold = rows // TILE
    return [
        pltpu.VMEM((size // 2 * TILE, 2 * size * fold), BF16),
        pltpu.VMEM((TILE // HALF, size * HALF, size * fold), F32),
        pltpu.VMEM((TILE // HALF, size * HALF, size * fold), F32),
    ]


def rotate(choice, inputs, constants, split=0):
    rows, width = inputs[0].shape
    fold = rows // TILE
    size = constants[1].shape[0] // HALF
    shapes = [jax.ShapeDtypeStruct((rows, width), BF16)]
    if split:
        shapes.append(jax.ShapeDtypeStruct((rows - split, width), BF16))
    return call(
        functools.partial(rotate_kernel, len(inputs), choice, split, PLACE),
        shapes,
        [IN_VMEM] * (len(inputs) + 5),
        turn_scratch(rows, constants),
        (*inputs, *constants),
        flops=8 * rows * width * size * fold,
        grant=12 << 20,
    )


def fill(held, units, choices, here_ref):
    at = 0
    for candidates, choice in zip(units, choices):
        rows = candidates[0].shape[0]

        def take(ref, at=at, rows=rows):
            held[at : at + rows, :] = ref[...]

        if len(candidates) == 1:
            take(candidates[0])
        else:
            which = lookup(choice, here_ref[0])
            for i, ref in enumerate(candidates):
                pl.when(which == i)(functools.partial(take, ref))
        at += rows


def products(held, x_ref, kept_ref):
    total = x_ref.shape[0]
    step = min(256, total)
    for t in range(0, total, step):
        kept_ref[:, t : t + step] = lax.dot_general(
            x_ref[t : t + step, :], held[...], (((1,), (1,)), ((), ())), preferred_element_type=F32
        ).T


def grid_lookup(table, z, owner):
    value = lookup([row[0] for row in table], z)
    for o in range(1, len(table[0])):
        value = jnp.where(owner == o, lookup([row[o] for row in table], z), value)
    return value


def aligned(start, rows):
    return pl.ds(pl.multiple_of(start, rows), rows)


def early_kernel(shape, choices, table, piece, raw_choice, here_ref, *refs):
    refs = list(refs)
    units = [[refs.pop(0) for _ in range(n)] for n in shape]
    x_ref = refs.pop(0)
    inputs = [refs.pop(0) for _ in range(len(set(raw_choice)))]
    constants = [refs.pop(0) for _ in range(5)]
    *scratch, held = refs[-4:]
    kept_ref, *sent = refs[:-4]
    fill(held, units, choices, here_ref)
    base = held.shape[0] - piece

    def write(row, lane, value):
        rows, lanes = value.shape
        held[base + row : base + row + rows, lane : lane + lanes] = value

    turn(inputs, raw_choice, here_ref, constants, scratch, write)
    products(held, x_ref, kept_ref)
    z, x = here_ref[0], here_ref[1]
    layers = len(sent) + 1
    for d, sent_ref in enumerate(sent, 1):
        target = lax.rem(x + d, layers)
        for p in range(len(table) - 1):
            start = grid_lookup(table[p], z, target)
            sent_ref[p * piece : (p + 1) * piece, :] = kept_ref[aligned(start, piece), :].astype(BF16)


def late_kernel(shape, choices, table, piece, here_ref, *refs):
    refs = list(refs)
    units = [[refs.pop(0) for _ in range(n)] for n in shape]
    x_ref, early_ref, kept_ref, *sent = refs[:-1]
    held = refs[-1]
    fill(held, units, choices, here_ref)
    products(held, x_ref, kept_ref)
    z, x = here_ref[0], here_ref[1]
    layers = len(sent) + 1
    for d, sent_ref in enumerate(sent, 1):
        start = grid_lookup(table[-1], z, lax.rem(x + d, layers))
        last = early_ref.shape[0]

        @pl.when(start == last)
        def _(sent_ref=sent_ref):
            sent_ref[...] = kept_ref[...].astype(BF16)

        @pl.when(start != last)
        def _(sent_ref=sent_ref, start=start):
            sent_ref[...] = early_ref[aligned(start, piece), :].astype(BF16)


def first_finish_kernel(table, places, piece, here_ref, early_ref, *refs):
    *received, out_ref = refs
    z, x = here_ref[0], here_ref[1]
    for p in range(len(table) - 1):
        value = early_ref[aligned(grid_lookup(table[p], z, x), piece), :]
        for ref in received:
            value = value + ref[p * piece : (p + 1) * piece, :].astype(F32)
        out_ref[aligned(grid_lookup(places[p], z, x), piece), :] = value


def last_finish_kernel(table, places, piece, here_ref, _, early_ref, late_ref, *refs):
    *received, out_ref, total, sem = refs
    z, x = here_ref[0], here_ref[1]
    start = grid_lookup(table[-1], z, x)
    last = early_ref.shape[0]
    other = received[0][...].astype(F32)
    for ref in received[1:]:
        other = other + ref[...].astype(F32)

    @pl.when(start == last)
    def _():
        total[...] = late_ref[...] + other

    @pl.when(start != last)
    def _():
        total[...] = early_ref[aligned(start, piece), :] + other

    place = aligned(grid_lookup(places[-1], z, x), piece)
    copy = pltpu.make_async_copy(total, out_ref.at[place], sem)
    copy.start()
    copy.wait()


def load_kernel(x_ref, out_ref, sem):
    pieces = sem.shape[0]
    step = x_ref.shape[0] // pieces
    copies = []
    for i in range(pieces):
        rows = pl.ds(i * step, step)
        copies.append(pltpu.make_async_copy(x_ref.at[rows], out_ref.at[rows], sem.at[i]))
    for copy in copies:
        copy.start()
    for copy in copies:
        copy.wait()


def resident(x):
    return pl.pallas_call(
        load_kernel,
        out_shape=pltpu.VMEM(x.shape, x.dtype),
        in_specs=[pl.BlockSpec(memory_space=pltpu.HBM)],
        out_specs=IN_VMEM,
        scratch_shapes=[pltpu.SemaphoreType.DMA((8,))],
        compiler_params=pltpu.CompilerParams(vmem_limit_bytes=12 << 20),
        cost_estimate=pl.CostEstimate(
            flops=0, bytes_accessed=2 * x.size * x.dtype.itemsize, transcendentals=0
        ),
    )(x)


def steps(train_grads, queries, bases, eigenvalues):
    blocks, layers, reps = lax.axis_size("blk"), lax.axis_size("layer"), lax.axis_size("rep")
    train = train_grads[0]
    own = queries[0, 0]
    base_rows, lanes = bases.shape[1:]
    size = lanes // 2
    rows = own.shape[0]
    fold = rows // TILE
    per_owner = blocks // layers

    plan, arrivals = line_plan(blocks)
    splits = 2
    piece = rows // splits

    raw, mixed = {}, {}
    raw[1, 1] = lax.ppermute(own, "blk", plan[1, 1])
    raw[1, 0] = lax.ppermute(own, "blk", plan[1, 0])

    eigen = eigenvalues.reshape(-1, lanes)
    eigen_rows = eigen.shape[0]
    packed = call(
        pack_kernel,
        jax.ShapeDtypeStruct((base_rows + eigen_rows, lanes), F32),
        [IN_VMEM] * 2,
        [],
        (bases[0], eigen),
        flops=0,
        grant=4 << 20,
    )
    pair = [packed]
    for e in range(1, reps):
        pair.append(lax.ppermute(packed, "rep", [(r, (r + e) % reps) for r in range(reps)]))
    pair = jnp.concatenate(pair, axis=0)
    parts = [pair]
    for d in range(1, blocks):
        parts.append(lax.ppermute(pair, "blk", [(a, (a + d) % blocks) for a in range(blocks)]))
    train, _ = lax.optimization_barrier((train, pair))
    train = resident(train)
    raw[1, 1], train = lax.optimization_barrier((raw[1, 1], train))
    raw[2, 0] = lax.ppermute(raw[1, 1], "blk", plan[2, 0])

    constants = rotation_constants(parts, reps, base_rows, eigen_rows, size, fold)
    alone = [0] * blocks
    block_of = [list(range(blocks))] + [[a[j][2] for a in arrivals] for j in range(blocks - 1)]
    source_of = [None] + [[a[j][:2] for a in arrivals] for j in range(blocks - 1)]

    def hop(step, parity, value):
        return lax.ppermute(value, "blk", plan[step, parity])

    mixed[2, 1] = [hop(2, 1, head(raw[1, 0], piece))] if (2, 1) in plan else []
    whole_first, last = rotate(alone, [raw[1, 0]], constants, piece)
    if mixed[2, 1]:
        mixed[2, 1].append(hop(2, 1, last))
        if (3, 0) in plan:
            mixed[3, 0] = [hop(3, 0, mixed[2, 1][0])]
    whole_own, = rotate(alone, [own], constants)
    units, choices = [[whole_own], [whole_first]], [alone, alone]

    turned_last = {}

    def last_rows(name):
        if name in mixed:
            return mixed[name][1]
        if name not in turned_last:
            turned_last[name] = rotate(alone, [raw[name]], constants, piece)[1]
        return turned_last[name]

    def first_rows(name):
        return mixed[name][0] if name in mixed else head(raw[name], piece)

    gate = whole_own
    late_raw = []
    for j in range(2, blocks):
        names = sorted(set(source_of[j]))
        choice = [names.index(s) for s in source_of[j]]
        if all(n in raw for n in names):
            whole, = rotate(choice, [raw[n] for n in names], constants)
            units.append([whole])
            choices.append(choice if len(units[-1]) > 1 else alone)
            gate = whole
            continue
        for step, parity in plan:
            if step > j or (step, parity) in raw:
                continue
            parts = mixed.setdefault((step, parity), [])
            before = (step - 1, 1 - parity)
            while len(parts) < splits:
                value = last_rows(before) if parts else first_rows(before)
                if step > 2:
                    value, _ = lax.optimization_barrier((value, gate))
                parts.append(hop(step, parity, value))
        late_raw.append((j, choice, [first_rows(n) for n in names]))
        units += [None, [last_rows(n) for n in names]]
        choices += [alone, choice]
    for j, choice, values in late_raw[:-1]:
        turned_piece, = rotate(choice, values, constants)
        units[units.index(None)] = [turned_piece]
    raw_choice, raw_values = late_raw[-1][1:]
    units.remove(None)
    choices.pop(-2)

    count = per_owner * splits
    table = [[[0] * layers for _ in range(blocks)] for _ in range(count)]
    places = [[[0] * layers for _ in range(blocks)] for _ in range(count)]
    for a in range(blocks):
        for o in range(layers):
            mine = [j for j in range(blocks) if block_of[j][a] // per_owner == o]
            for p in range(count):
                j, part = mine[p // splits], p % splits
                table[p][a][o] = j * rows + part * piece
                places[p][a][o] = block_of[j][a] % per_owner * rows + part * piece

    def shifted(sent):
        return [
            lax.ppermute(s, "layer", [(o, (o + d) % layers) for o in range(layers)])
            for d, s in enumerate(sent, 1)
        ]

    total, width = train.shape

    def scores(kernel, units, choices, extra, held, sent_rows, scratch, grant):
        flat = [w for u in units for w in u] + [train] + extra
        sent_shape = jax.ShapeDtypeStruct((sent_rows, total), BF16)
        return call(
            functools.partial(kernel, [len(u) for u in units], choices, table, piece, PLACE),
            [jax.ShapeDtypeStruct((held, total), F32)] + [sent_shape] * (layers - 1),
            [IN_VMEM] * len(flat),
            scratch + [pltpu.VMEM((held, width), BF16)],
            tuple(flat),
            flops=2 * held * total * width,
            grant=grant,
        )

    early, *sent = scores(
        lambda shape, choices, table, piece, *refs: early_kernel(
            shape, choices, table, piece, raw_choice, *refs
        ),
        units[:-1],
        choices[:-1],
        [*raw_values, *constants],
        blocks * rows - piece,
        (count - 1) * piece,
        turn_scratch(piece, constants),
        16 << 20,
    )
    first = shifted(sent)
    late, *sent = scores(
        late_kernel, units[-1:], choices[-1:], [early], piece, piece, [], 12 << 20
    )
    second = shifted(sent)
    out_shape = jax.ShapeDtypeStruct((per_owner * rows, total), F32)
    out = call(
        functools.partial(first_finish_kernel, table, places, piece, PLACE),
        out_shape,
        [IN_VMEM] * layers,
        [],
        (early, *first),
        flops=per_owner * rows * total,
        grant=8 << 20,
    )
    in_hbm = pl.BlockSpec(memory_space=pltpu.HBM)
    out = pl.pallas_call(
        functools.partial(last_finish_kernel, table, places, piece, PLACE),
        out_shape=out_shape,
        in_specs=[in_hbm] + [IN_VMEM] * (1 + layers),
        out_specs=in_hbm,
        scratch_shapes=[pltpu.VMEM((piece, total), F32), pltpu.SemaphoreType.DMA],
        input_output_aliases={0: 0},
        compiler_params=pltpu.CompilerParams(vmem_limit_bytes=8 << 20),
    )(out, early, late, *second)
    return out[None]


def solution(mesh):
    return jax.shard_map(
        steps,
        mesh=mesh,
        in_specs=(
            P("layer", ("groups", "blk"), None),
            P("layer", "rep", ("groups", "blk"), None),
            P("layer", ("blk", "rep"), None),
            P("layer", ("blk", "rep")),
        ),
        out_specs=P("rep", "layer", ("groups", "blk")),
        check_vma=False,
    )
```

```python
import functools
import math

import jax
import jax.numpy as jnp
from jax import lax
from jax.experimental import pallas as pl
from jax.experimental.pallas import tpu as pltpu
from jax.sharding import PartitionSpec as P

TILE = 16
HALF = 8
BF16, F32 = jnp.bfloat16, jnp.float32
IN_VMEM = pl.BlockSpec(memory_space=pltpu.VMEM)
IN_HBM = pl.BlockSpec(memory_space=pltpu.HBM)


class Place:
    def __getitem__(self, axis):
        return lax.axis_index(("blk", "layer", "rep")[axis])


PLACE = Place()


def dot(a, b):
    return jnp.dot(a, b, preferred_element_type=F32)


def call(kernel, out_shape, in_specs, scratch, args, flops, grant):
    outs = out_shape if isinstance(out_shape, (list, tuple)) else [out_shape]
    moved = sum(math.prod(a.shape) * a.dtype.itemsize for a in list(args) + list(outs))
    return pl.pallas_call(
        kernel,
        out_shape=out_shape,
        in_specs=in_specs,
        out_specs=[IN_VMEM] * len(outs) if outs is out_shape else IN_VMEM,
        scratch_shapes=scratch,
        compiler_params=pltpu.CompilerParams(vmem_limit_bytes=grant),
        cost_estimate=pl.CostEstimate(flops=flops, bytes_accessed=moved, transcendentals=0),
    )(*args)


def line_plan(count):
    plan, arrivals = {}, [[] for _ in range(count)]
    for step in range(1, count):
        for parity in range(2):
            pairs = []
            for low in range(parity, count - 1, 2):
                high = low + 1
                if low - (step - 1) >= 0:
                    pairs.append((low, high))
                    arrivals[high].append((step, parity, low - (step - 1)))
                if high + (step - 1) < count:
                    pairs.append((high, low))
                    arrivals[low].append((step, parity, high + (step - 1)))
            if pairs:
                plan[step, parity] = pairs
    return plan, arrivals


def lookup(values, index):
    value = jnp.int32(values[0])
    for i, v in enumerate(values[1:], 1):
        if v != values[0]:
            value = jnp.where(index == i, jnp.int32(v), value)
    return value


def spread(matrix, rows, cols, keep):
    size = matrix.shape[0]
    r = lax.broadcasted_iota(jnp.int32, (rows, size), 0)
    i = lax.broadcasted_iota(jnp.int32, (rows, size), 1)
    j = lax.broadcasted_iota(jnp.int32, (size, cols), 0)
    c = lax.broadcasted_iota(jnp.int32, (size, cols), 1)
    down = jnp.where(lax.rem(r, size) == i, 1.0, 0.0).astype(BF16)
    along = jnp.where(lax.rem(c, size) == j, 1.0, 0.0).astype(BF16)
    full = dot(dot(down, matrix.astype(BF16)).astype(BF16), along)
    block_row = lax.broadcasted_iota(jnp.int32, (rows, cols), 0) // size
    block_col = lax.broadcasted_iota(jnp.int32, (rows, cols), 1) // size
    return jnp.where(keep(block_row, block_col), full, 0.0).astype(BF16)


def comb(matrix, out_ref):
    size = matrix.shape[0]
    wide = size * HALF
    j = lax.broadcasted_iota(jnp.int32, (size, wide), 0)
    c = lax.broadcasted_iota(jnp.int32, (size, wide), 1)
    rows = dot(matrix.astype(BF16), jnp.where(c // HALF == j, 1.0, 0.0).astype(BF16))
    r = lax.broadcasted_iota(jnp.int32, (HALF, wide), 0)
    c = lax.broadcasted_iota(jnp.int32, (HALF, wide), 1)
    keep = r == lax.rem(c, HALF)
    for i in range(0, size, 2):
        pair = [
            jnp.where(keep, jnp.broadcast_to(rows[k : k + 1], (HALF, wide)), 0.0) for k in (i, i + 1)
        ]
        out_ref[i * HALF : (i + 2) * HALF, :] = jnp.concatenate(pair, axis=0).astype(BF16)


def prep_kernel(shape, here_ref, *refs):
    count, reps, base_rows, eigen_rows, fold = shape
    parts, train_ref, refs = refs[:count], refs[count], refs[count + 1 :]
    w1_ref, but_ref, bu_ref, w5_ref, inv_ref, x_ref, base3, eigen3, base, eigen, pad, sem = refs
    load = pltpu.make_async_copy(train_ref.at[pl.ds(0, x_ref.shape[0])], x_ref, sem)
    load.start()
    z, rep = here_ref[0], here_ref[2]
    each = base_rows + eigen_rows
    for d in range(count):
        for e in range(reps):
            source = lax.rem(z + count - d, count) * reps + lax.rem(rep + reps - e, reps)
            base3[source] = parts[d][e * each : e * each + base_rows, :]
            eigen3[source] = parts[d][e * each + base_rows : (e + 1) * each, :]
    for s in range(count * reps):
        base[s * base_rows : (s + 1) * base_rows, :] = base3[s]
        eigen[s * eigen_rows : (s + 1) * eigen_rows, :] = eigen3[s]
    size = base.shape[0]
    basis = base[...]
    left, right = basis[:, :size], basis[:, size:]
    turned = basis.T
    left_t, right_t = turned[:size], turned[size:]
    wide = 2 * size * fold
    w1_ref[...] = spread(
        right, wide, wide, lambda r, c: (r // 2 == lax.rem(c, fold)) & (lax.rem(r, 2) == c // fold)
    )
    w5_ref[...] = spread(
        right_t, wide, wide, lambda r, c: (c // 2 == lax.rem(r, fold)) & (lax.rem(c, 2) == r // fold)
    )
    comb(left_t, but_ref)
    comb(left, bu_ref)
    values = eigen[...]
    inverse = 1.0 / (values + 0.1 * (jnp.sum(values) / (size * size)))
    shifted = pltpu.roll(inverse, size, 1)
    lane = lax.broadcasted_iota(jnp.int32, inverse.shape, 1)
    pad[pl.ds(0, size // 2, stride=2), :] = jnp.where(lane < size, inverse, shifted)
    pad[pl.ds(1, size // 2, stride=2), :] = jnp.where(lane < size, shifted, inverse)
    for i in range(size):
        row = jnp.broadcast_to(pad[i : i + 1, :], (HALF, 2 * size))
        for h in range(fold // 2):
            inv_ref[i * HALF : (i + 1) * HALF, h * 2 * size : (h + 1) * 2 * size] = row
    load.wait()


def rotation_constants(parts, train, taken, reps, base_rows, eigen_rows, size, fold):
    count = len(parts)
    wide, tall = 2 * size * fold, HALF * size
    shard = count * reps
    return call(
        functools.partial(prep_kernel, (count, reps, base_rows, eigen_rows, fold), PLACE),
        [
            jax.ShapeDtypeStruct((wide, wide), BF16),
            jax.ShapeDtypeStruct((tall, tall), BF16),
            jax.ShapeDtypeStruct((tall, tall), BF16),
            jax.ShapeDtypeStruct((wide, wide), BF16),
            jax.ShapeDtypeStruct((tall, size * fold), F32),
            pltpu.VMEM((taken, train.shape[1]), train.dtype),
        ],
        [IN_VMEM] * count + [IN_HBM],
        [
            pltpu.VMEM((shard, base_rows, 2 * size), F32),
            pltpu.VMEM((shard, eigen_rows, 2 * size), F32),
            pltpu.VMEM((size, 2 * size), F32),
            pltpu.VMEM((size // 2, 2 * size), F32),
            pltpu.VMEM((size, 2 * size), F32),
            pltpu.SemaphoreType.DMA,
        ],
        (*parts, pltpu.with_memory_space_constraint(train, pltpu.HBM)),
        flops=2 * wide * wide * 2 * size,
        grant=12 << 20,
    )


def pack_kernel(bases_ref, eigen_ref, out_ref):
    rows = bases_ref.shape[0]
    out_ref[:rows, :] = bases_ref[...].astype(F32)
    out_ref[rows:, :] = eigen_ref[...]


def head_kernel(rows_ref, out_ref):
    out_ref[...] = rows_ref[: out_ref.shape[0], :]


def head(value, rows):
    shape = jax.ShapeDtypeStruct((rows, value.shape[1]), value.dtype)
    return call(head_kernel, shape, [IN_VMEM], [], (value,), flops=0, grant=4 << 20)


def turn(inputs, choice, here_ref, constants, scratch, write):
    w1_ref, but_ref, bu_ref, w5_ref, inv_ref = constants
    tall, first, second = scratch
    size = but_ref.shape[0] // HALF
    lanes = 2 * size
    fold = inputs[0].shape[0] // TILE
    pairs = size // 2
    half = size * fold

    def gather_rows(q_ref):
        for a in range(pairs):
            for h in range(fold):
                tall[a * TILE : (a + 1) * TILE, h * lanes : (h + 1) * lanes] = q_ref[
                    h * TILE : (h + 1) * TILE, a * lanes : (a + 1) * lanes
                ]

    if len(inputs) == 1:
        gather_rows(inputs[0])
    else:
        which = lookup(choice, here_ref[0])
        for i in range(len(inputs)):
            pl.when(which == i)(functools.partial(gather_rows, inputs[i]))
    full = w1_ref.shape[0] // 2
    if half == full:
        w1, w5, inverse = w1_ref[...], w5_ref[...], inv_ref[...]
    else:
        wide = fold * lanes
        w1 = jnp.concatenate([w1_ref[:wide, k * full : k * full + half] for k in range(2)], axis=1)
        w5 = jnp.concatenate([w5_ref[k * full : k * full + half, :wide] for k in range(2)], axis=0)
        inverse = inv_ref[:, :half]
    chunk = 8
    parts = TILE // HALF
    for a0 in range(0, pairs, chunk):
        rows = dot(tall[a0 * TILE : (a0 + chunk) * TILE, :], w1)
        for a in range(a0, a0 + chunk):
            for part in range(parts):
                low = (a - a0) * TILE + part * HALF
                for odd in range(2):
                    at = (2 * a + odd) * HALF
                    first[part, at : at + HALF, :] = rows[low : low + HALF, odd * half : (odd + 1) * half]
    but, bu = but_ref[...], bu_ref[...]
    for part in range(parts):
        scaled = (dot(but, first[part].astype(BF16)) * inverse).astype(BF16)
        second[part] = dot(bu, scaled)
    for a in range(pairs):
        for odd in range(2):
            at = (2 * a + odd) * HALF
            value = jnp.concatenate([second[part, at : at + HALF, :] for part in range(parts)], axis=0)
            tall[a * TILE : (a + 1) * TILE, odd * half : (odd + 1) * half] = value.astype(BF16)
    for a0 in range(0, pairs, chunk):
        rows = dot(tall[a0 * TILE : (a0 + chunk) * TILE, :], w5).astype(BF16)
        for a in range(a0, a0 + chunk):
            for h in range(fold):
                value = rows[(a - a0) * TILE : (a - a0 + 1) * TILE, h * lanes : (h + 1) * lanes]
                write(h * TILE, a * lanes, value)


def rotate_kernel(sources, choice, split, start, here_ref, *refs):
    inputs, refs = refs[:sources], refs[sources:]
    constants, refs = refs[:5], list(refs[5:])
    load = None
    if start is not None:
        train_ref, sem = refs.pop(0), refs.pop()
        x_ref = refs.pop(2 if split else 1)
        load = pltpu.make_async_copy(train_ref.at[pl.ds(start, x_ref.shape[0])], x_ref, sem)
        load.start()
    out_ref, *rest = refs

    def write(row, lane, value):
        rows, lanes = value.shape
        out_ref[row : row + rows, lane : lane + lanes] = value
        if split and row >= split:
            rest[0][row - split : row - split + rows, lane : lane + lanes] = value

    turn(inputs, choice, here_ref, constants, rest[-3:], write)
    if load is not None:
        load.wait()


def turn_scratch(rows, constants):
    size = constants[1].shape[0] // HALF
    fold = rows // TILE
    return [
        pltpu.VMEM((size // 2 * TILE, 2 * size * fold), BF16),
        pltpu.VMEM((TILE // HALF, size * HALF, size * fold), F32),
        pltpu.VMEM((TILE // HALF, size * HALF, size * fold), F32),
    ]


def rotate(choice, inputs, constants, split=0, load=None):
    rows, width = inputs[0].shape
    fold = rows // TILE
    size = constants[1].shape[0] // HALF
    shapes = [jax.ShapeDtypeStruct((rows, width), BF16)]
    if split:
        shapes.append(jax.ShapeDtypeStruct((rows - split, width), BF16))
    specs, args = [IN_VMEM] * (len(inputs) + 5), [*inputs, *constants]
    scratch, start = turn_scratch(rows, constants), None
    if load is not None:
        array, start, taken = load
        shapes.append(pltpu.VMEM((taken, array.shape[1]), array.dtype))
        specs.append(IN_HBM)
        args.append(pltpu.with_memory_space_constraint(array, pltpu.HBM))
        scratch = scratch + [pltpu.SemaphoreType.DMA]
    return call(
        functools.partial(rotate_kernel, len(inputs), choice, split, start, PLACE),
        shapes,
        specs,
        scratch,
        tuple(args),
        flops=8 * rows * width * size * fold,
        grant=16 << 20,
    )


def fill(held, units, choices, here_ref):
    at = 0
    for candidates, choice in zip(units, choices):
        rows = candidates[0].shape[0]

        def take(ref, at=at, rows=rows):
            held[at : at + rows, :] = ref[...]

        if len(candidates) == 1:
            take(candidates[0])
        else:
            which = lookup(choice, here_ref[0])
            for i, ref in enumerate(candidates):
                pl.when(which == i)(functools.partial(take, ref))
        at += rows


def products(held, x_refs, kept_ref):
    at = 0
    for x_ref in x_refs:
        total = x_ref.shape[0]
        kept_ref[:, at : at + total] = lax.dot_general(
            x_ref[...], held[...], (((1,), (1,)), ((), ())), preferred_element_type=F32
        ).T
        at += total


def grid_lookup(table, z, owner):
    value = lookup([row[0] for row in table], z)
    for o in range(1, len(table[0])):
        value = jnp.where(owner == o, lookup([row[o] for row in table], z), value)
    return value


def aligned(start, rows):
    return pl.ds(pl.multiple_of(start, rows), rows)


def early_kernel(shape, choices, table, piece, loaded, raw_choice, here_ref, *refs):
    refs = list(refs)
    units = [[refs.pop(0) for _ in range(n)] for n in shape]
    x_refs = [refs.pop(0) for _ in range(loaded)]
    inputs = [refs.pop(0) for _ in range(len(set(raw_choice)))]
    constants = [refs.pop(0) for _ in range(5)]
    *scratch, held = refs[-4:]
    kept_ref, *sent = refs[:-4]
    fill(held, units, choices, here_ref)
    base = held.shape[0] - piece

    def write(row, lane, value):
        rows, lanes = value.shape
        held[base + row : base + row + rows, lane : lane + lanes] = value

    turn(inputs, raw_choice, here_ref, constants, scratch, write)
    products(held, x_refs, kept_ref)
    z, x = here_ref[0], here_ref[1]
    layers = len(sent) + 1
    for d, sent_ref in enumerate(sent, 1):
        target = lax.rem(x + d, layers)
        for p in range(len(table) - 1):
            start = grid_lookup(table[p], z, target)
            sent_ref[p * piece : (p + 1) * piece, :] = kept_ref[aligned(start, piece), :].astype(BF16)


def late_kernel(shape, choices, table, piece, loaded, here_ref, *refs):
    refs = list(refs)
    units = [[refs.pop(0) for _ in range(n)] for n in shape]
    x_refs = [refs.pop(0) for _ in range(loaded)]
    early_ref, kept_ref, *sent = refs[:-1]
    held = refs[-1]
    fill(held, units, choices, here_ref)
    products(held, x_refs, kept_ref)
    z, x = here_ref[0], here_ref[1]
    layers = len(sent) + 1
    for d, sent_ref in enumerate(sent, 1):
        start = grid_lookup(table[-1], z, lax.rem(x + d, layers))
        last = early_ref.shape[0]

        @pl.when(start == last)
        def _(sent_ref=sent_ref):
            sent_ref[...] = kept_ref[...].astype(BF16)

        @pl.when(start != last)
        def _(sent_ref=sent_ref, start=start):
            sent_ref[...] = early_ref[aligned(start, piece), :].astype(BF16)


def first_finish_kernel(table, places, piece, here_ref, early_ref, *refs):
    *received, out_ref = refs
    z, x = here_ref[0], here_ref[1]
    for p in range(len(table) - 1):
        value = early_ref[aligned(grid_lookup(table[p], z, x), piece), :]
        for ref in received:
            value = value + ref[p * piece : (p + 1) * piece, :].astype(F32)
        out_ref[aligned(grid_lookup(places[p], z, x), piece), :] = value


def last_finish_kernel(table, places, piece, here_ref, _, early_ref, late_ref, *refs):
    *received, out_ref, total, sem = refs
    z, x = here_ref[0], here_ref[1]
    start = grid_lookup(table[-1], z, x)
    last = early_ref.shape[0]
    other = received[0][...].astype(F32)
    for ref in received[1:]:
        other = other + ref[...].astype(F32)

    @pl.when(start == last)
    def _():
        total[...] = late_ref[...] + other

    @pl.when(start != last)
    def _():
        total[...] = early_ref[aligned(start, piece), :] + other

    place = aligned(grid_lookup(places[-1], z, x), piece)
    copy = pltpu.make_async_copy(total, out_ref.at[place], sem)
    copy.start()
    copy.wait()


def steps(train_grads, queries, bases, eigenvalues):
    blocks, layers, reps = lax.axis_size("blk"), lax.axis_size("layer"), lax.axis_size("rep")
    train = train_grads[0]
    own = queries[0, 0]
    base_rows, lanes = bases.shape[1:]
    size = lanes // 2
    rows = own.shape[0]
    fold = rows // TILE
    per_owner = blocks // layers

    plan, arrivals = line_plan(blocks)
    splits = 2
    piece = rows // splits

    raw, mixed = {}, {}
    raw[1, 1] = lax.ppermute(own, "blk", plan[1, 1])
    raw[1, 0] = lax.ppermute(own, "blk", plan[1, 0])

    eigen = eigenvalues.reshape(-1, lanes)
    eigen_rows = eigen.shape[0]
    packed = call(
        pack_kernel,
        jax.ShapeDtypeStruct((base_rows + eigen_rows, lanes), F32),
        [IN_VMEM] * 2,
        [],
        (bases[0], eigen),
        flops=0,
        grant=4 << 20,
    )
    pair = [packed]
    for e in range(1, reps):
        pair.append(lax.ppermute(packed, "rep", [(r, (r + e) % reps) for r in range(reps)]))
    pair = jnp.concatenate(pair, axis=0)
    parts = [pair]
    for d in range(1, blocks):
        parts.append(lax.ppermute(pair, "blk", [(a, (a + d) % blocks) for a in range(blocks)]))
    raw[2, 0] = lax.ppermute(raw[1, 1], "blk", plan[2, 0])

    quarter = train.shape[0] // 4
    *constants, loaded = rotation_constants(
        parts, train, quarter, reps, base_rows, eigen_rows, size, fold
    )
    loaded = [loaded]
    alone = [0] * blocks
    block_of = [list(range(blocks))] + [[a[j][2] for a in arrivals] for j in range(blocks - 1)]
    source_of = [None] + [[a[j][:2] for a in arrivals] for j in range(blocks - 1)]

    def hop(step, parity, value):
        return lax.ppermute(value, "blk", plan[step, parity])

    mixed[2, 1] = [hop(2, 1, head(raw[1, 0], piece))] if (2, 1) in plan else []
    whole_first, last, part = rotate(
        alone, [raw[1, 0]], constants, piece, (train, quarter, quarter)
    )
    loaded.append(part)
    if mixed[2, 1]:
        mixed[2, 1].append(hop(2, 1, last))
        if (3, 0) in plan:
            mixed[3, 0] = [hop(3, 0, mixed[2, 1][0])]
    whole_own, part = rotate(alone, [own], constants, 0, (train, 2 * quarter, quarter))
    loaded.append(part)
    units, choices = [[whole_own], [whole_first]], [alone, alone]

    turned_last = {}

    def last_rows(name):
        if name in mixed:
            return mixed[name][1]
        if name not in turned_last:
            turned_last[name] = rotate(alone, [raw[name]], constants, piece)[1]
        return turned_last[name]

    def first_rows(name):
        return mixed[name][0] if name in mixed else head(raw[name], piece)

    gate = whole_own
    late_raw = []
    for j in range(2, blocks):
        names = sorted(set(source_of[j]))
        choice = [names.index(s) for s in source_of[j]]
        if all(n in raw for n in names):
            whole, part = rotate(
                choice, [raw[n] for n in names], constants, 0, (train, 3 * quarter, quarter)
            )
            loaded.append(part)
            units.append([whole])
            choices.append(choice if len(units[-1]) > 1 else alone)
            gate = whole
            continue
        for step, parity in plan:
            if step > j or (step, parity) in raw:
                continue
            parts = mixed.setdefault((step, parity), [])
            before = (step - 1, 1 - parity)
            while len(parts) < splits:
                value = last_rows(before) if parts else first_rows(before)
                if step > 2:
                    value, _ = lax.optimization_barrier((value, gate))
                parts.append(hop(step, parity, value))
        late_raw.append((j, choice, [first_rows(n) for n in names]))
        units += [None, [last_rows(n) for n in names]]
        choices += [alone, choice]
    for j, choice, values in late_raw[:-1]:
        turned_piece, = rotate(choice, values, constants)
        units[units.index(None)] = [turned_piece]
    raw_choice, raw_values = late_raw[-1][1:]
    units.remove(None)
    choices.pop(-2)

    count = per_owner * splits
    table = [[[0] * layers for _ in range(blocks)] for _ in range(count)]
    places = [[[0] * layers for _ in range(blocks)] for _ in range(count)]
    for a in range(blocks):
        for o in range(layers):
            mine = [j for j in range(blocks) if block_of[j][a] // per_owner == o]
            for p in range(count):
                j, part = mine[p // splits], p % splits
                table[p][a][o] = j * rows + part * piece
                places[p][a][o] = block_of[j][a] % per_owner * rows + part * piece

    def shifted(sent):
        return [
            lax.ppermute(s, "layer", [(o, (o + d) % layers) for o in range(layers)])
            for d, s in enumerate(sent, 1)
        ]

    total, width = train.shape

    def scores(kernel, units, choices, extra, held, sent_rows, scratch, grant):
        flat = [w for u in units for w in u] + loaded + extra
        sent_shape = jax.ShapeDtypeStruct((sent_rows, total), BF16)
        return call(
            functools.partial(kernel, [len(u) for u in units], choices, table, piece, len(loaded), PLACE),
            [jax.ShapeDtypeStruct((held, total), F32)] + [sent_shape] * (layers - 1),
            [IN_VMEM] * len(flat),
            scratch + [pltpu.VMEM((held, width), BF16)],
            tuple(flat),
            flops=2 * held * total * width,
            grant=grant,
        )

    early, *sent = scores(
        lambda shape, choices, table, piece, loaded, *refs: early_kernel(
            shape, choices, table, piece, loaded, raw_choice, *refs
        ),
        units[:-1],
        choices[:-1],
        [*raw_values, *constants],
        blocks * rows - piece,
        (count - 1) * piece,
        turn_scratch(piece, constants),
        16 << 20,
    )
    first = shifted(sent)
    late, *sent = scores(
        late_kernel, units[-1:], choices[-1:], [early], piece, piece, [], 12 << 20
    )
    second = shifted(sent)
    out_shape = jax.ShapeDtypeStruct((per_owner * rows, total), F32)
    out = call(
        functools.partial(first_finish_kernel, table, places, piece, PLACE),
        out_shape,
        [IN_VMEM] * layers,
        [],
        (early, *first),
        flops=per_owner * rows * total,
        grant=8 << 20,
    )
    out = pl.pallas_call(
        functools.partial(last_finish_kernel, table, places, piece, PLACE),
        out_shape=out_shape,
        in_specs=[IN_HBM] + [IN_VMEM] * (1 + layers),
        out_specs=IN_HBM,
        scratch_shapes=[pltpu.VMEM((piece, total), F32), pltpu.SemaphoreType.DMA],
        input_output_aliases={0: 0},
        compiler_params=pltpu.CompilerParams(vmem_limit_bytes=8 << 20),
    )(out, early, late, *second)
    return out[None]


def solution(mesh):
    return jax.shard_map(
        steps,
        mesh=mesh,
        in_specs=(
            P("layer", ("groups", "blk"), None),
            P("layer", "rep", ("groups", "blk"), None),
            P("layer", ("blk", "rep"), None),
            P("layer", ("blk", "rep")),
        ),
        out_specs=P("rep", "layer", ("groups", "blk")),
        check_vma=False,
    )
```

```python
import functools
import math

import jax
import jax.numpy as jnp
from jax import lax
from jax.experimental import pallas as pl
from jax.experimental.pallas import tpu as pltpu
from jax.sharding import PartitionSpec as P

TILE = 16
HALF = 8
BF16, F32 = jnp.bfloat16, jnp.float32
IN_VMEM = pl.BlockSpec(memory_space=pltpu.VMEM)
IN_HBM = pl.BlockSpec(memory_space=pltpu.HBM)


class Place:
    def __getitem__(self, axis):
        return lax.axis_index(("blk", "layer", "rep")[axis])


PLACE = Place()


def dot(a, b):
    return jnp.dot(a, b, preferred_element_type=F32)


def call(kernel, out_shape, in_specs, scratch, args, flops, grant):
    outs = out_shape if isinstance(out_shape, (list, tuple)) else [out_shape]
    moved = sum(math.prod(a.shape) * a.dtype.itemsize for a in list(args) + list(outs))
    return pl.pallas_call(
        kernel,
        out_shape=out_shape,
        in_specs=in_specs,
        out_specs=[IN_VMEM] * len(outs) if outs is out_shape else IN_VMEM,
        scratch_shapes=scratch,
        compiler_params=pltpu.CompilerParams(vmem_limit_bytes=grant),
        cost_estimate=pl.CostEstimate(flops=flops, bytes_accessed=moved, transcendentals=0),
    )(*args)


def line_plan(count):
    plan, arrivals = {}, [[] for _ in range(count)]
    for step in range(1, count):
        for parity in range(2):
            pairs = []
            for low in range(parity, count - 1, 2):
                high = low + 1
                if low - (step - 1) >= 0:
                    pairs.append((low, high))
                    arrivals[high].append((step, parity, low - (step - 1)))
                if high + (step - 1) < count:
                    pairs.append((high, low))
                    arrivals[low].append((step, parity, high + (step - 1)))
            if pairs:
                plan[step, parity] = pairs
    return plan, arrivals


def lookup(values, index):
    value = jnp.int32(values[0])
    for i, v in enumerate(values[1:], 1):
        if v != values[0]:
            value = jnp.where(index == i, jnp.int32(v), value)
    return value


def spread(matrix, rows, cols, keep):
    size = matrix.shape[0]
    r = lax.broadcasted_iota(jnp.int32, (rows, size), 0)
    i = lax.broadcasted_iota(jnp.int32, (rows, size), 1)
    j = lax.broadcasted_iota(jnp.int32, (size, cols), 0)
    c = lax.broadcasted_iota(jnp.int32, (size, cols), 1)
    down = jnp.where(lax.rem(r, size) == i, 1.0, 0.0).astype(BF16)
    along = jnp.where(lax.rem(c, size) == j, 1.0, 0.0).astype(BF16)
    full = dot(dot(down, matrix.astype(BF16)).astype(BF16), along)
    block_row = lax.broadcasted_iota(jnp.int32, (rows, cols), 0) // size
    block_col = lax.broadcasted_iota(jnp.int32, (rows, cols), 1) // size
    return jnp.where(keep(block_row, block_col), full, 0.0).astype(BF16)


def comb(matrix, out_ref):
    size = matrix.shape[0]
    wide = size * HALF
    j = lax.broadcasted_iota(jnp.int32, (size, wide), 0)
    c = lax.broadcasted_iota(jnp.int32, (size, wide), 1)
    rows = dot(matrix.astype(BF16), jnp.where(c // HALF == j, 1.0, 0.0).astype(BF16))
    r = lax.broadcasted_iota(jnp.int32, (HALF, wide), 0)
    c = lax.broadcasted_iota(jnp.int32, (HALF, wide), 1)
    keep = r == lax.rem(c, HALF)
    for i in range(0, size, 2):
        pair = [
            jnp.where(keep, jnp.broadcast_to(rows[k : k + 1], (HALF, wide)), 0.0) for k in (i, i + 1)
        ]
        out_ref[i * HALF : (i + 2) * HALF, :] = jnp.concatenate(pair, axis=0).astype(BF16)


def prep_kernel(shape, here_ref, *refs):
    count, reps, base_rows, eigen_rows, fold = shape
    parts, train_ref, refs = refs[:count], refs[count], refs[count + 1 :]
    w1_ref, but_ref, bu_ref, w5_ref, inv_ref, x_ref, base3, eigen3, base, eigen, pad, sem = refs
    load = pltpu.make_async_copy(train_ref.at[pl.ds(0, x_ref.shape[0])], x_ref, sem)
    load.start()
    z, rep = here_ref[0], here_ref[2]
    each = base_rows + eigen_rows
    for d in range(count):
        for e in range(reps):
            source = lax.rem(z + count - d, count) * reps + lax.rem(rep + reps - e, reps)
            base3[source] = parts[d][e * each : e * each + base_rows, :]
            eigen3[source] = parts[d][e * each + base_rows : (e + 1) * each, :]
    for s in range(count * reps):
        base[s * base_rows : (s + 1) * base_rows, :] = base3[s]
        eigen[s * eigen_rows : (s + 1) * eigen_rows, :] = eigen3[s]
    size = base.shape[0]
    basis = base[...]
    left, right = basis[:, :size], basis[:, size:]
    turned = basis.T
    left_t, right_t = turned[:size], turned[size:]
    wide = 2 * size * fold
    w1_ref[...] = spread(
        right, wide, wide, lambda r, c: (r // 2 == lax.rem(c, fold)) & (lax.rem(r, 2) == c // fold)
    )
    w5_ref[...] = spread(
        right_t, wide, wide, lambda r, c: (c // 2 == lax.rem(r, fold)) & (lax.rem(c, 2) == r // fold)
    )
    comb(left_t, but_ref)
    comb(left, bu_ref)
    values = eigen[...]
    inverse = 1.0 / (values + 0.1 * (jnp.sum(values) / (size * size)))
    shifted = pltpu.roll(inverse, size, 1)
    lane = lax.broadcasted_iota(jnp.int32, inverse.shape, 1)
    pad[pl.ds(0, size // 2, stride=2), :] = jnp.where(lane < size, inverse, shifted)
    pad[pl.ds(1, size // 2, stride=2), :] = jnp.where(lane < size, shifted, inverse)
    for i in range(size):
        row = jnp.broadcast_to(pad[i : i + 1, :], (HALF, 2 * size))
        for h in range(fold // 2):
            inv_ref[i * HALF : (i + 1) * HALF, h * 2 * size : (h + 1) * 2 * size] = row
    load.wait()


def rotation_constants(parts, train, taken, reps, base_rows, eigen_rows, size, fold):
    count = len(parts)
    wide, tall = 2 * size * fold, HALF * size
    shard = count * reps
    return call(
        functools.partial(prep_kernel, (count, reps, base_rows, eigen_rows, fold), PLACE),
        [
            jax.ShapeDtypeStruct((wide, wide), BF16),
            jax.ShapeDtypeStruct((tall, tall), BF16),
            jax.ShapeDtypeStruct((tall, tall), BF16),
            jax.ShapeDtypeStruct((wide, wide), BF16),
            jax.ShapeDtypeStruct((tall, size * fold), F32),
            pltpu.VMEM((taken, train.shape[1]), train.dtype),
        ],
        [IN_VMEM] * count + [IN_HBM],
        [
            pltpu.VMEM((shard, base_rows, 2 * size), F32),
            pltpu.VMEM((shard, eigen_rows, 2 * size), F32),
            pltpu.VMEM((size, 2 * size), F32),
            pltpu.VMEM((size // 2, 2 * size), F32),
            pltpu.VMEM((size, 2 * size), F32),
            pltpu.SemaphoreType.DMA,
        ],
        (*parts, pltpu.with_memory_space_constraint(train, pltpu.HBM)),
        flops=2 * wide * wide * 2 * size,
        grant=12 << 20,
    )


def pack_kernel(bases_ref, eigen_ref, out_ref):
    rows = bases_ref.shape[0]
    out_ref[:rows, :] = bases_ref[...].astype(F32)
    out_ref[rows:, :] = eigen_ref[...]


def head_kernel(rows_ref, out_ref):
    out_ref[...] = rows_ref[: out_ref.shape[0], :]


def head(value, rows):
    shape = jax.ShapeDtypeStruct((rows, value.shape[1]), value.dtype)
    return call(head_kernel, shape, [IN_VMEM], [], (value,), flops=0, grant=4 << 20)


def turn(inputs, choice, here_ref, constants, scratch, write, beside=None):
    w1_ref, but_ref, bu_ref, w5_ref, inv_ref = constants
    tall, first, second = scratch
    size = but_ref.shape[0] // HALF
    lanes = 2 * size
    fold = inputs[0].shape[0] // TILE
    pairs = size // 2
    half = size * fold

    def gather_rows(q_ref):
        for a in range(pairs):
            for h in range(fold):
                tall[a * TILE : (a + 1) * TILE, h * lanes : (h + 1) * lanes] = q_ref[
                    h * TILE : (h + 1) * TILE, a * lanes : (a + 1) * lanes
                ]

    if len(inputs) == 1:
        gather_rows(inputs[0])
    else:
        which = lookup(choice, here_ref[0])
        for i in range(len(inputs)):
            pl.when(which == i)(functools.partial(gather_rows, inputs[i]))
    if beside is not None:
        beside()
    full = w1_ref.shape[0] // 2
    if half == full:
        w1, w5 = w1_ref[...], w5_ref[...]
    else:
        wide = fold * lanes
        w1 = jnp.concatenate([w1_ref[:wide, k * full : k * full + half] for k in range(2)], axis=1)
        w5 = jnp.concatenate([w5_ref[k * full : k * full + half, :wide] for k in range(2)], axis=0)
    chunk = 8
    parts = TILE // HALF
    for a0 in range(0, pairs, chunk):
        rows = dot(tall[a0 * TILE : (a0 + chunk) * TILE, :], w1)
        for a in range(a0, a0 + chunk):
            for part in range(parts):
                low = (a - a0) * TILE + part * HALF
                for odd in range(2):
                    at = (2 * a + odd) * HALF
                    first[part, at : at + HALF, :] = rows[low : low + HALF, odd * half : (odd + 1) * half]
    but, bu = but_ref[...], bu_ref[...]
    joined = parts if parts * half <= full else 1
    for low in range(0, parts, joined):
        both = jnp.concatenate([first[low + k].astype(BF16) for k in range(joined)], axis=1)
        scaled = (dot(but, both) * inv_ref[:, : joined * half]).astype(BF16)
        back = dot(bu, scaled)
        for k in range(joined):
            second[low + k] = back[:, k * half : (k + 1) * half]
    for a in range(pairs):
        for odd in range(2):
            at = (2 * a + odd) * HALF
            value = jnp.concatenate([second[part, at : at + HALF, :] for part in range(parts)], axis=0)
            tall[a * TILE : (a + 1) * TILE, odd * half : (odd + 1) * half] = value.astype(BF16)
    for a0 in range(0, pairs, chunk):
        rows = dot(tall[a0 * TILE : (a0 + chunk) * TILE, :], w5).astype(BF16)
        for a in range(a0, a0 + chunk):
            for h in range(fold):
                value = rows[(a - a0) * TILE : (a - a0 + 1) * TILE, h * lanes : (h + 1) * lanes]
                write(h * TILE, a * lanes, value)


def rotate_kernel(sources, choice, split, start, here_ref, *refs):
    inputs, refs = refs[:sources], refs[sources:]
    constants, refs = refs[:5], list(refs[5:])
    load = None
    if start is not None:
        train_ref, sem = refs.pop(0), refs.pop()
        x_ref = refs.pop(2 if split else 1)
        load = pltpu.make_async_copy(train_ref.at[pl.ds(start, x_ref.shape[0])], x_ref, sem)
        load.start()
    out_ref, *rest = refs

    def write(row, lane, value):
        rows, lanes = value.shape
        out_ref[row : row + rows, lane : lane + lanes] = value
        if split and row >= split:
            rest[0][row - split : row - split + rows, lane : lane + lanes] = value

    turn(inputs, choice, here_ref, constants, rest[-3:], write)
    if load is not None:
        load.wait()


def turn_scratch(rows, constants):
    size = constants[1].shape[0] // HALF
    fold = rows // TILE
    return [
        pltpu.VMEM((size // 2 * TILE, 2 * size * fold), BF16),
        pltpu.VMEM((TILE // HALF, size * HALF, size * fold), F32),
        pltpu.VMEM((TILE // HALF, size * HALF, size * fold), F32),
    ]


def rotate(choice, inputs, constants, split=0, load=None):
    rows, width = inputs[0].shape
    fold = rows // TILE
    size = constants[1].shape[0] // HALF
    shapes = [jax.ShapeDtypeStruct((rows, width), BF16)]
    if split:
        shapes.append(jax.ShapeDtypeStruct((rows - split, width), BF16))
    specs, args = [IN_VMEM] * (len(inputs) + 5), [*inputs, *constants]
    scratch, start = turn_scratch(rows, constants), None
    if load is not None:
        array, start, taken = load
        shapes.append(pltpu.VMEM((taken, array.shape[1]), array.dtype))
        specs.append(IN_HBM)
        args.append(pltpu.with_memory_space_constraint(array, pltpu.HBM))
        scratch = scratch + [pltpu.SemaphoreType.DMA]
    return call(
        functools.partial(rotate_kernel, len(inputs), choice, split, start, PLACE),
        shapes,
        specs,
        scratch,
        tuple(args),
        flops=8 * rows * width * size * fold,
        grant=16 << 20,
    )


def fill(held, units, choices, here_ref):
    at = 0
    for candidates, choice in zip(units, choices):
        rows = candidates[0].shape[0]

        def take(ref, at=at, rows=rows):
            held[at : at + rows, :] = ref[...]

        if len(candidates) == 1:
            take(candidates[0])
        else:
            which = lookup(choice, here_ref[0])
            for i, ref in enumerate(candidates):
                pl.when(which == i)(functools.partial(take, ref))
        at += rows


def products(held, x_refs, kept_ref):
    at = 0
    for x_ref in x_refs:
        total = x_ref.shape[0]
        kept_ref[:, at : at + total] = lax.dot_general(
            x_ref[...], held[...], (((1,), (1,)), ((), ())), preferred_element_type=F32
        ).T
        at += total


def grid_lookup(table, z, owner):
    value = lookup([row[0] for row in table], z)
    for o in range(1, len(table[0])):
        value = jnp.where(owner == o, lookup([row[o] for row in table], z), value)
    return value


def aligned(start, rows):
    return pl.ds(pl.multiple_of(start, rows), rows)


def early_kernel(shape, choices, table, piece, loaded, raw_choice, here_ref, *refs):
    refs = list(refs)
    units = [[refs.pop(0) for _ in range(n)] for n in shape]
    x_refs = [refs.pop(0) for _ in range(loaded)]
    inputs = [refs.pop(0) for _ in range(len(set(raw_choice)))]
    constants = [refs.pop(0) for _ in range(5)]
    *scratch, held = refs[-4:]
    kept_ref, *sent = refs[:-4]
    base = held.shape[0] - piece

    def write(row, lane, value):
        rows, lanes = value.shape
        held[base + row : base + row + rows, lane : lane + lanes] = value

    beside = functools.partial(fill, held, units, choices, here_ref)
    turn(inputs, raw_choice, here_ref, constants, scratch, write, beside)
    products(held, x_refs, kept_ref)
    z, x = here_ref[0], here_ref[1]
    layers = len(sent) + 1
    for d, sent_ref in enumerate(sent, 1):
        target = lax.rem(x + d, layers)
        for p in range(len(table) - 1):
            start = grid_lookup(table[p], z, target)
            sent_ref[p * piece : (p + 1) * piece, :] = kept_ref[aligned(start, piece), :].astype(BF16)


def late_kernel(shape, choices, table, piece, loaded, here_ref, *refs):
    refs = list(refs)
    units = [[refs.pop(0) for _ in range(n)] for n in shape]
    x_refs = [refs.pop(0) for _ in range(loaded)]
    early_ref, kept_ref, *sent = refs[:-1]
    held = refs[-1]
    fill(held, units, choices, here_ref)
    products(held, x_refs, kept_ref)
    z, x = here_ref[0], here_ref[1]
    layers = len(sent) + 1
    for d, sent_ref in enumerate(sent, 1):
        start = grid_lookup(table[-1], z, lax.rem(x + d, layers))
        last = early_ref.shape[0]

        @pl.when(start == last)
        def _(sent_ref=sent_ref):
            sent_ref[...] = kept_ref[...].astype(BF16)

        @pl.when(start != last)
        def _(sent_ref=sent_ref, start=start):
            sent_ref[...] = early_ref[aligned(start, piece), :].astype(BF16)


def first_finish_kernel(table, places, piece, here_ref, early_ref, *refs):
    *received, out_ref = refs
    z, x = here_ref[0], here_ref[1]
    for p in range(len(table) - 1):
        value = early_ref[aligned(grid_lookup(table[p], z, x), piece), :]
        for ref in received:
            value = value + ref[p * piece : (p + 1) * piece, :].astype(F32)
        out_ref[aligned(grid_lookup(places[p], z, x), piece), :] = value


def last_finish_kernel(table, places, piece, here_ref, _, early_ref, late_ref, *refs):
    *received, out_ref, total, sem = refs
    z, x = here_ref[0], here_ref[1]
    start = grid_lookup(table[-1], z, x)
    last = early_ref.shape[0]
    other = received[0][...].astype(F32)
    for ref in received[1:]:
        other = other + ref[...].astype(F32)

    @pl.when(start == last)
    def _():
        total[...] = late_ref[...] + other

    @pl.when(start != last)
    def _():
        total[...] = early_ref[aligned(start, piece), :] + other

    place = aligned(grid_lookup(places[-1], z, x), piece)
    copy = pltpu.make_async_copy(total, out_ref.at[place], sem)
    copy.start()
    copy.wait()


def steps(train_grads, queries, bases, eigenvalues):
    blocks, layers, reps = lax.axis_size("blk"), lax.axis_size("layer"), lax.axis_size("rep")
    train = train_grads[0]
    own = queries[0, 0]
    base_rows, lanes = bases.shape[1:]
    size = lanes // 2
    rows = own.shape[0]
    fold = rows // TILE
    per_owner = blocks // layers

    plan, arrivals = line_plan(blocks)
    splits = 2
    piece = rows // splits

    raw, mixed = {}, {}
    raw[1, 1] = lax.ppermute(own, "blk", plan[1, 1])
    raw[1, 0] = lax.ppermute(own, "blk", plan[1, 0])

    eigen = eigenvalues.reshape(-1, lanes)
    eigen_rows = eigen.shape[0]
    packed = call(
        pack_kernel,
        jax.ShapeDtypeStruct((base_rows + eigen_rows, lanes), F32),
        [IN_VMEM] * 2,
        [],
        (bases[0], eigen),
        flops=0,
        grant=4 << 20,
    )
    pair = [packed]
    for e in range(1, reps):
        pair.append(lax.ppermute(packed, "rep", [(r, (r + e) % reps) for r in range(reps)]))
    pair = jnp.concatenate(pair, axis=0)
    parts = [pair]
    for d in range(1, blocks):
        parts.append(lax.ppermute(pair, "blk", [(a, (a + d) % blocks) for a in range(blocks)]))
    raw[2, 0] = lax.ppermute(raw[1, 1], "blk", plan[2, 0])

    quarter = train.shape[0] // 4
    *constants, loaded = rotation_constants(
        parts, train, quarter, reps, base_rows, eigen_rows, size, fold
    )
    loaded = [loaded]
    alone = [0] * blocks
    block_of = [list(range(blocks))] + [[a[j][2] for a in arrivals] for j in range(blocks - 1)]
    source_of = [None] + [[a[j][:2] for a in arrivals] for j in range(blocks - 1)]

    def hop(step, parity, value):
        return lax.ppermute(value, "blk", plan[step, parity])

    mixed[2, 1] = [hop(2, 1, head(raw[1, 0], piece))] if (2, 1) in plan else []
    whole_first, last, part = rotate(
        alone, [raw[1, 0]], constants, piece, (train, quarter, quarter)
    )
    loaded.append(part)
    if mixed[2, 1]:
        mixed[2, 1].append(hop(2, 1, last))
        if (3, 0) in plan:
            mixed[3, 0] = [hop(3, 0, mixed[2, 1][0])]
    whole_own, part = rotate(alone, [own], constants, 0, (train, 2 * quarter, quarter))
    loaded.append(part)
    units, choices = [[whole_own], [whole_first]], [alone, alone]

    turned_last = {}

    def last_rows(name):
        if name in mixed:
            return mixed[name][1]
        if name not in turned_last:
            turned_last[name] = rotate(alone, [raw[name]], constants, piece)[1]
        return turned_last[name]

    def first_rows(name):
        return mixed[name][0] if name in mixed else head(raw[name], piece)

    gate = whole_own
    late_raw = []
    for j in range(2, blocks):
        names = sorted(set(source_of[j]))
        choice = [names.index(s) for s in source_of[j]]
        if all(n in raw for n in names):
            whole, part = rotate(
                choice, [raw[n] for n in names], constants, 0, (train, 3 * quarter, quarter)
            )
            loaded.append(part)
            units.append([whole])
            choices.append(choice if len(units[-1]) > 1 else alone)
            gate = whole
            continue
        for step, parity in plan:
            if step > j or (step, parity) in raw:
                continue
            parts = mixed.setdefault((step, parity), [])
            before = (step - 1, 1 - parity)
            while len(parts) < splits:
                value = last_rows(before) if parts else first_rows(before)
                if step > 2:
                    value, _ = lax.optimization_barrier((value, gate))
                parts.append(hop(step, parity, value))
        late_raw.append((j, choice, [first_rows(n) for n in names]))
        units += [None, [last_rows(n) for n in names]]
        choices += [alone, choice]
    for j, choice, values in late_raw[:-1]:
        turned_piece, = rotate(choice, values, constants)
        units[units.index(None)] = [turned_piece]
    raw_choice, raw_values = late_raw[-1][1:]
    units.remove(None)
    choices.pop(-2)

    count = per_owner * splits
    table = [[[0] * layers for _ in range(blocks)] for _ in range(count)]
    places = [[[0] * layers for _ in range(blocks)] for _ in range(count)]
    for a in range(blocks):
        for o in range(layers):
            mine = [j for j in range(blocks) if block_of[j][a] // per_owner == o]
            for p in range(count):
                j, part = mine[p // splits], p % splits
                table[p][a][o] = j * rows + part * piece
                places[p][a][o] = block_of[j][a] % per_owner * rows + part * piece

    def shifted(sent):
        return [
            lax.ppermute(s, "layer", [(o, (o + d) % layers) for o in range(layers)])
            for d, s in enumerate(sent, 1)
        ]

    total, width = train.shape

    def scores(kernel, units, choices, extra, held, sent_rows, scratch, grant):
        flat = [w for u in units for w in u] + loaded + extra
        sent_shape = jax.ShapeDtypeStruct((sent_rows, total), BF16)
        return call(
            functools.partial(kernel, [len(u) for u in units], choices, table, piece, len(loaded), PLACE),
            [jax.ShapeDtypeStruct((held, total), F32)] + [sent_shape] * (layers - 1),
            [IN_VMEM] * len(flat),
            scratch + [pltpu.VMEM((held, width), BF16)],
            tuple(flat),
            flops=2 * held * total * width,
            grant=grant,
        )

    early, *sent = scores(
        lambda shape, choices, table, piece, loaded, *refs: early_kernel(
            shape, choices, table, piece, loaded, raw_choice, *refs
        ),
        units[:-1],
        choices[:-1],
        [*raw_values, *constants],
        blocks * rows - piece,
        (count - 1) * piece,
        turn_scratch(piece, constants),
        16 << 20,
    )
    first = shifted(sent)
    late, *sent = scores(
        late_kernel, units[-1:], choices[-1:], [early], piece, piece, [], 12 << 20
    )
    second = shifted(sent)
    out_shape = jax.ShapeDtypeStruct((per_owner * rows, total), F32)
    out = call(
        functools.partial(first_finish_kernel, table, places, piece, PLACE),
        out_shape,
        [IN_VMEM] * layers,
        [],
        (early, *first),
        flops=per_owner * rows * total,
        grant=8 << 20,
    )
    out = pl.pallas_call(
        functools.partial(last_finish_kernel, table, places, piece, PLACE),
        out_shape=out_shape,
        in_specs=[IN_HBM] + [IN_VMEM] * (1 + layers),
        out_specs=IN_HBM,
        scratch_shapes=[pltpu.VMEM((piece, total), F32), pltpu.SemaphoreType.DMA],
        input_output_aliases={0: 0},
        compiler_params=pltpu.CompilerParams(vmem_limit_bytes=8 << 20),
    )(out, early, late, *second)
    return out[None]


def solution(mesh):
    return jax.shard_map(
        steps,
        mesh=mesh,
        in_specs=(
            P("layer", ("groups", "blk"), None),
            P("layer", "rep", ("groups", "blk"), None),
            P("layer", ("blk", "rep"), None),
            P("layer", ("blk", "rep")),
        ),
        out_specs=P("rep", "layer", ("groups", "blk")),
        check_vma=False,
    )
```
